32 devices in a mesh: slab: 16 (over z, x, core), tp: 2 (over y).
Axes of the slice: x: 2, y: 2, z: 4, core: 2. Of those that a mesh axis runs over, the one named last changes fastest.
Arguments:
- tokens: bfloat16 [16384, 512], P('slab', 'tp'), may hold values from -8 to 8
- stem_taps: float32 [3, 512], P(None, 'tp'), may hold values from 0.1 to 1.9
- query_weight: bfloat16 [512, 512], P(None, 'tp'), may hold values from -0.25 to 0.25
- key_weight: bfloat16 [512, 512], P(None, 'tp'), may hold values from -0.25 to 0.25
- value_weight: bfloat16 [512, 512], P(None, 'tp'), may hold values from -0.25 to 0.25
- out_weight: bfloat16 [512, 512], P('tp'), may hold values from -0.25 to 0.25
- key_blocks: int32 [128, 4], P('slab'), may hold values from 0 to 127, as said below
- counts: int32 [128], P('slab'), may hold values from 3 to 4, as said below
- cotangent: bfloat16 [16384, 512], P('slab', 'tp'), may hold values from -6 to 6
Outputs:
- layer_out: bfloat16 [16384, 512], P('slab', 'tp')
- grad_tokens: float32 [16384, 512], P('slab', 'tp')
- grad_taps: float32 [3, 512], P(None, 'tp')
- grad_query_weight: float32 [512, 512], P(None, 'tp')
- grad_key_weight: float32 [512, 512], P(None, 'tp')
- grad_value_weight: float32 [512, 512], P(None, 'tp')
- grad_out_weight: float32 [512, 512], P('tp')
The draws below stay inside these ranges and needn't reach their ends.
Inputs may be any that keep to these rules, and one draw needn't show every extreme that they name: `key_blocks`: query block i lies in plane p = i // 4. Its slots 0, 1, 2 name the block at the same position in planes p, p - 1 and p + 1 (planes modulo 32); every live slot names a different block of these three planes; slots from counts[i] on name block i itself. `counts`: some query block has all 4 slots live; loads differ from plane to plane.
All inputs are finite; a program needn't handle non-finite values.
Results may differ from the reference program's by a relative error of at most 0.009.
The reference program's roundings to bfloat16 on the way count: a program that leaves them out, or rounds other values in their place, can miss the bound.
Values may be sent and summed in bfloat16 or wider, within the bound.
A program may use at most 128 MiB of HBM per device.

```python
import jax
import jax.numpy as jnp
from jax import lax

D = 512
HEADS = 8
HD = 64
BLK = 128
PLANE_TOK = 512
MAXK = 4
TOKENS = 16384
NPLANES = 32


def draw_tokens(key, part):
    key_normal = jax.random.fold_in(key, 0)
    values = jax.random.normal(key_normal, (TOKENS, D), jnp.float32)
    return jnp.clip(values, -8.0, 8.0).astype(jnp.bfloat16)


def shared_pattern(key):
    pattern_key = jax.random.fold_in(key, 11)
    key_rank, key_cap, key_count = jax.random.split(pattern_key, 3)
    per_plane = PLANE_TOK // BLK
    block_total = NPLANES * per_plane
    query_ids = jnp.arange(block_total, dtype=jnp.int32)
    plane_ids = query_ids // per_plane
    block_pos = query_ids % per_plane

    def rank_row(row_key):
        return jax.random.permutation(row_key, 3 * per_plane)
    rank_rows = jax.vmap(rank_row)(jax.random.split(key_rank, block_total)).astype(jnp.int32)
    candidate = jnp.arange(3 * per_plane, dtype=jnp.int32)[None, :]
    priority = jnp.where(candidate == per_plane + block_pos[:, None], -3, jnp.where(candidate == block_pos[:, None], -2, jnp.where(candidate == 2 * per_plane + block_pos[:, None], -1, rank_rows)))
    slot_order = jnp.argsort(priority, axis=1)[:, :MAXK].astype(jnp.int32)
    key_plane = jnp.remainder(plane_ids[:, None] + slot_order // per_plane - 1, NPLANES)
    chosen = key_plane * per_plane + slot_order % per_plane
    plane_caps = jax.random.randint(key_cap, (NPLANES,), 3, MAXK + 1)
    live_counts = 3 + jax.random.randint(key_count, (block_total,), 0, plane_caps[plane_ids] - 2)
    live_counts = live_counts.at[0].set(MAXK)
    slot_ids = jnp.arange(MAXK, dtype=jnp.int32)[None, :]
    chosen = jnp.where(slot_ids < live_counts[:, None], chosen, query_ids[:, None])
    return (chosen.astype(jnp.int32), live_counts.astype(jnp.int32))


def draw_key_blocks(key, part):
    return shared_pattern(key)[0]


def draw_counts(key, part):
    return shared_pattern(key)[1]


def level_of(key, extent, shards, smallest, high):
    level, own = 1.0, jax.random.fold_in(key, 6)
    for axis_at, blocks in shards:
        heights = jnp.exp(jax.random.uniform(jax.random.fold_in(own, axis_at), (blocks,), jnp.float32, smallest / len(shards), high / len(shards)))
        level = level * jnp.repeat(heights, extent[axis_at] // blocks).reshape([-1 if axis == axis_at else 1 for axis in range(len(extent))])
    return level


def gaussian(stream_key, dims, spread, most, cuts=(), kind=jnp.bfloat16):
    result = jax.random.normal(stream_key, dims, jnp.float32) * spread
    if len(cuts) > 0:
        result = level_of(stream_key, dims, cuts, -0.22, 0.18) * result
    return jnp.clip(result, min=-most, max=most).astype(kind)


def setup_inputs(seed: int = 0) -> dict:
    key_list = jax.random.split(jax.random.key(seed), 10)
    return {
        "tokens": draw_tokens(jax.random.fold_in(key_list[9], 71), 0),
        "stem_taps": jnp.clip(1.0 + 0.18 * jax.random.normal(key_list[1], (3, D), jnp.float32), 0.1, 1.9),
        "query_weight": gaussian(key_list[2], (D, D), D ** -0.5, 0.25, ((1, 2),)),
        "key_weight": gaussian(key_list[3], (D, D), D ** -0.5, 0.25, ((1, 2),)),
        "value_weight": gaussian(key_list[4], (D, D), D ** -0.5, 0.25, ((1, 2),)),
        "out_weight": gaussian(key_list[5], (D, D), D ** -0.5, 0.25, ((0, 2),)),
        "key_blocks": draw_key_blocks(jax.random.fold_in(key_list[9], 71), 0),
        "counts": draw_counts(jax.random.fold_in(key_list[9], 71), 0),
        "cotangent": gaussian(key_list[8], (TOKENS, D), 1.0, 6.0, ((0, 16), (1, 2))),
    }


NEG = -1e30


def softmax_scores(query_block, key_block, live_counts):
    scores = jnp.einsum("gqhd,gkhd->ghqk", query_block, key_block) * (HD ** -0.5)
    slot_ids = jnp.arange(key_block.shape[1]) // BLK
    live_mask = slot_ids[None, :] < live_counts[:, None]
    scores = jnp.where(live_mask[:, None, None, :], scores, NEG)
    row_max = jnp.max(scores, axis=-1, keepdims=True)
    exp_scores = jnp.exp(scores - row_max)
    return exp_scores / jnp.sum(exp_scores, axis=-1, keepdims=True)


def reference(tokens, stem_taps, query_weight, key_weight, value_weight, out_weight, key_blocks, counts, cotangent):
    inputs_f = tokens.astype(jnp.float32)
    before_rows = jnp.roll(inputs_f, PLANE_TOK, axis=0)
    after_rows = jnp.roll(inputs_f, -PLANE_TOK, axis=0)
    stem_rows = (stem_taps[0] * before_rows + stem_taps[1] * inputs_f + stem_taps[2] * after_rows).astype(jnp.bfloat16)
    query_rows = jnp.dot(stem_rows, query_weight, preferred_element_type=jnp.float32).astype(jnp.bfloat16)
    key_rows = jnp.dot(stem_rows, key_weight, preferred_element_type=jnp.float32).astype(jnp.bfloat16)
    value_rows = jnp.dot(stem_rows, value_weight, preferred_element_type=jnp.float32).astype(jnp.bfloat16)
    block_total = TOKENS // BLK
    groups = block_total // 4
    key_all = key_rows.reshape(block_total, BLK, HEADS, HD)
    value_all = value_rows.reshape(block_total, BLK, HEADS, HD)
    query_groups = query_rows.reshape(groups, 4, BLK, HEADS, HD)
    index_groups = key_blocks.reshape(groups, 4, MAXK).astype(jnp.int32)
    count_groups = counts.reshape(groups, 4)

    def fetch(table, block_ids):
        picked = jnp.take(table, block_ids.reshape(-1), axis=0)
        return picked.reshape(4, MAXK * BLK, HEADS, HD).astype(jnp.float32)

    def forward_group(inputs):
        query_block, block_ids, live_counts = inputs
        key_block = fetch(key_all, block_ids)
        value_block = fetch(value_all, block_ids)
        attn_probs = softmax_scores(query_block.astype(jnp.float32), key_block, live_counts)
        probs_low = lax.optimization_barrier(attn_probs.astype(jnp.bfloat16)).astype(jnp.float32)
        return jnp.einsum("ghqk,gkhd->gqhd", probs_low, value_block).astype(jnp.bfloat16)

    attn = lax.map(forward_group, (query_groups, index_groups, count_groups)).reshape(TOKENS, D)
    mixed_rows = jnp.dot(attn, out_weight, preferred_element_type=jnp.float32)
    layer_out = (stem_rows.astype(jnp.float32) + mixed_rows).astype(jnp.bfloat16)

    grad_attn = jnp.dot(cotangent, out_weight.T, preferred_element_type=jnp.float32).astype(jnp.bfloat16)
    grad_out_weight = jnp.dot(attn.T, cotangent, preferred_element_type=jnp.float32)
    grad_groups = grad_attn.reshape(groups, 4, BLK, HEADS, HD)

    def backward_group(grad_pairs, inputs):
        query_block, block_ids, live_counts, grad_block = inputs
        query_f = query_block.astype(jnp.float32)
        grad_f = grad_block.astype(jnp.float32)
        key_block = fetch(key_all, block_ids)
        value_block = fetch(value_all, block_ids)
        attn_probs = softmax_scores(query_f, key_block, live_counts)
        probs_low = lax.optimization_barrier(attn_probs.astype(jnp.bfloat16)).astype(jnp.float32)
        grad_probs = jnp.einsum("gqhd,gkhd->ghqk", grad_f, value_block)
        row_inner = jnp.sum(attn_probs * grad_probs, axis=-1, keepdims=True)
        grad_scores = attn_probs * (grad_probs - row_inner) * (HD ** -0.5)
        grad_scores = lax.optimization_barrier(grad_scores.astype(jnp.bfloat16)).astype(jnp.float32)
        grad_query = jnp.einsum("ghqk,gkhd->gqhd", grad_scores, key_block).astype(jnp.bfloat16)
        grad_key = jnp.einsum("ghqk,gqhd->gkhd", grad_scores, query_f)
        grad_value = jnp.einsum("ghqk,gqhd->gkhd", probs_low, grad_f)
        slot_rows = jnp.stack([grad_key, grad_value]).reshape(2, 4 * MAXK, BLK, D)
        grad_pairs = grad_pairs.at[:, block_ids.reshape(-1)].add(slot_rows)
        return grad_pairs, grad_query

    start_pairs = jnp.zeros((2, block_total, BLK, D), jnp.float32)
    grad_pairs, grad_query = lax.scan(backward_group, start_pairs, (query_groups, index_groups, count_groups, grad_groups))
    grad_query = grad_query.reshape(TOKENS, D)
    grad_key = grad_pairs[0].reshape(TOKENS, D).astype(jnp.bfloat16)
    grad_value = grad_pairs[1].reshape(TOKENS, D).astype(jnp.bfloat16)
    grad_stem = cotangent.astype(jnp.float32) + (jnp.dot(grad_query, query_weight.T, preferred_element_type=jnp.float32) + jnp.dot(grad_key, key_weight.T, preferred_element_type=jnp.float32) + jnp.dot(grad_value, value_weight.T, preferred_element_type=jnp.float32))
    grad_tokens = stem_taps[0] * jnp.roll(grad_stem, -PLANE_TOK, axis=0) + stem_taps[1] * grad_stem + stem_taps[2] * jnp.roll(grad_stem, PLANE_TOK, axis=0)
    grad_taps = jnp.stack([jnp.sum(grad_stem * before_rows, axis=0), jnp.sum(grad_stem * inputs_f, axis=0), jnp.sum(grad_stem * after_rows, axis=0)])
    grad_query_weight = jnp.dot(stem_rows.T, grad_query, preferred_element_type=jnp.float32)
    grad_key_weight = jnp.dot(stem_rows.T, grad_key, preferred_element_type=jnp.float32)
    grad_value_weight = jnp.dot(stem_rows.T, grad_value, preferred_element_type=jnp.float32)
    return (layer_out, grad_tokens, grad_taps, grad_query_weight, grad_key_weight, grad_value_weight, grad_out_weight)
```

```python
import functools

import jax
import jax.numpy as jnp
from jax import lax
from jax.experimental import pallas as pl
from jax.experimental.pallas import tpu as pltpu
from jax.sharding import PartitionSpec as P

HD = 64
BLK = 128
PLANE_TOK = 512
MAXK = 4
NEG = -1e30
F32 = jnp.float32
BF16 = jnp.bfloat16
MESH = pl.DeviceIdType.MESH
VMEM = pl.BlockSpec(memory_space=pltpu.VMEM)
SMEM = pl.BlockSpec(memory_space=pltpu.SMEM)
ANY = pl.BlockSpec(memory_space=pl.ANY)
LIMIT = 60 * 1024 * 1024
CHUNK = 256


def mm(a, b):
    return jnp.dot(a, b, preferred_element_type=F32)


def mm_nt(a, b):
    return lax.dot_general(a, b, (((1,), (1,)), ((), ())), preferred_element_type=F32)


def mm_tn(a, b):
    return lax.dot_general(a, b, (((0,), (0,)), ((), ())), preferred_element_type=F32)


def part(index, width):
    return pl.ds(pl.multiple_of(index * width, width), width)


def project_kernel(so_ref, st_ref, wq_ref, wk_ref, wv_ref, q_ref, kv_ref):
    tp = lax.axis_index("tp")
    width = so_ref.shape[1]
    cols = wq_ref.shape[1]
    mine, other = part(tp, width), part(1 - tp, width)

    @pl.loop(0, so_ref.shape[0] // CHUNK)
    def _(step):
        rows = part(step, CHUNK)
        so, st = so_ref[rows, :], st_ref[rows, :]

        def project(w_ref):
            return (mm(so, w_ref[mine, :]) + mm(st, w_ref[other, :])).astype(BF16)

        q_ref[rows, :] = project(wq_ref)
        kv_ref[rows, 0:cols] = project(wk_ref)
        kv_ref[rows, cols : 2 * cols] = project(wv_ref)


def attention_kernel(
    slabs,
    blocks_ref,
    counts_ref,
    q_ref,
    kv_ref,
    kv_prev_ref,
    kv_next_ref,
    co_ref,
    ct_ref,
    ow_ref,
    gq_ref,
    gkv_ref,
    gprev_ref,
    gnext_ref,
    mix_ref,
    mix_other_ref,
    gow_ref,
    ext,
    acc,
    grad,
    attn,
    sems,
):
    tp = lax.axis_index("tp")
    slab = lax.axis_index("slab")
    tokens, cols = q_ref.shape
    width = co_ref.shape[1]
    heads = cols // HD
    planes = tokens // PLANE_TOK
    per_plane = PLANE_TOK // BLK
    total = planes * slabs
    copies = [
        pltpu.make_async_copy(kv_prev_ref, ext.at[0:PLANE_TOK], sems.at[0]),
        pltpu.make_async_copy(kv_ref, ext.at[PLANE_TOK : PLANE_TOK + tokens], sems.at[1]),
        pltpu.make_async_copy(
            kv_next_ref, ext.at[PLANE_TOK + tokens : 2 * PLANE_TOK + tokens], sems.at[2]
        ),
    ]
    for copy in copies:
        copy.start()
    mine, other = part(tp, width), part(1 - tp, width)

    @pl.loop(0, tokens // CHUNK)
    def _(step):
        rows = part(step, CHUNK)
        grad[rows, :] = (
            mm_nt(co_ref[rows, :], ow_ref[:, mine]) + mm_nt(ct_ref[rows, :], ow_ref[:, other])
        ).astype(BF16)

    @pl.loop(0, acc.shape[0] // BLK)
    def _(step):
        acc[part(step, BLK), :] = jnp.zeros((BLK, 2 * cols), F32)

    for copy in copies:
        copy.wait()

    lane = lax.broadcasted_iota(jnp.int32, (1, cols), 1) // HD
    masks = [(lane == h).astype(F32).astype(BF16) for h in range(heads)]
    slot = lax.broadcasted_iota(jnp.int32, (1, MAXK * BLK), 1)

    def stack(block):
        return jnp.concatenate([block * mask for mask in masks], axis=0)

    def pick(value):
        out = value[0:BLK]
        for h in range(1, heads):
            out = jnp.where(lane == h, value[h * BLK : (h + 1) * BLK], out)
        return out

    @pl.loop(0, tokens // BLK)
    def _(i):
        rows = part(i, BLK)
        where = []
        for j in range(MAXK):
            block = blocks_ref[i, j]
            plane = lax.rem(
                lax.div(block, per_plane) - slab * planes + 1 + total, total
            )
            where.append(part(plane * per_plane + lax.rem(block, per_plane), BLK))
        keys = jnp.concatenate([ext[at, 0:cols] for at in where], axis=0)
        values = jnp.concatenate([ext[at, cols : 2 * cols] for at in where], axis=0)
        queries = stack(q_ref[rows, :] * jnp.asarray(HD**-0.5, BF16))
        grads = stack(grad[rows, :])
        scores = mm_nt(queries, keys)
        scores = jnp.where(slot < counts_ref[i] * BLK, scores, NEG)
        exps = jnp.exp(scores - jnp.max(scores, axis=-1, keepdims=True))
        probs = exps * (1.0 / jnp.sum(exps, axis=-1, keepdims=True))
        low = probs.astype(BF16)
        attn[rows, :] = pick(mm(low, values)).astype(BF16)
        gprobs = mm_nt(grads, values)
        inner = jnp.sum(probs * gprobs, axis=-1, keepdims=True)
        gscores = (probs * (gprobs - inner)).astype(BF16)
        gq_ref[rows, :] = (pick(mm(gscores, keys)) * (HD**-0.5)).astype(BF16)
        gkeys = mm_tn(gscores, queries)
        gvalues = mm_tn(low, grads)
        for j in range(MAXK):
            acc[where[j], 0:cols] += gkeys[j * BLK : (j + 1) * BLK]
            acc[where[j], cols : 2 * cols] += gvalues[j * BLK : (j + 1) * BLK]

    gprev_ref[...] = acc[0:PLANE_TOK, :].astype(BF16)
    gkv_ref[...] = acc[PLANE_TOK : PLANE_TOK + tokens, :]
    gnext_ref[...] = acc[PLANE_TOK + tokens : 2 * PLANE_TOK + tokens, :].astype(BF16)

    @pl.loop(0, tokens // CHUNK)
    def _(step):
        rows = part(step, CHUNK)
        mix_ref[rows, :] = mm(attn[rows, :], ow_ref[:, mine])
        mix_other_ref[rows, :] = mm(attn[rows, :], ow_ref[:, other]).astype(BF16)

    halves = width // 128
    for index, c_ref in ((tp, co_ref), (1 - tp, ct_ref)):
        product = mm_tn(attn[...], c_ref[...])
        for half in range(halves):
            gow_ref[part(index * halves + half, cols), :] = product[
                :, half * 128 : (half + 1) * 128
            ]


def gradient_kernel(
    gq_ref,
    gkv_ref,
    from_prev_ref,
    from_next_ref,
    so_ref,
    st_ref,
    wq_ref,
    wk_ref,
    wv_ref,
    part_ref,
    part_other_ref,
    gw_ref,
    low,
):
    tp = lax.axis_index("tp")
    tokens, cols = gq_ref.shape
    width = so_ref.shape[1]
    depth = wq_ref.shape[0]
    mine, other = part(tp, width), part(1 - tp, width)
    low[...] = gkv_ref[...].astype(BF16)
    last = tokens - PLANE_TOK
    if last > 0:
        low[0:PLANE_TOK, :] = (gkv_ref[0:PLANE_TOK, :] + from_prev_ref[...].astype(F32)).astype(
            BF16
        )
        low[last:, :] = (gkv_ref[last:, :] + from_next_ref[...].astype(F32)).astype(BF16)
    else:
        low[...] = (
            gkv_ref[...] + from_prev_ref[...].astype(F32) + from_next_ref[...].astype(F32)
        ).astype(BF16)

    @pl.loop(0, tokens // CHUNK)
    def _(step):
        rows = part(step, CHUNK)
        gq = gq_ref[rows, :]
        gk = low[rows, 0:cols]
        gv = low[rows, cols : 2 * cols]

        def back(at):
            return (
                mm_nt(gq, wq_ref[at, :]) + mm_nt(gk, wk_ref[at, :]) + mm_nt(gv, wv_ref[at, :])
            )

        part_ref[rows, :] = back(mine)
        part_other_ref[rows, :] = back(other).astype(BF16)

    halves = cols // 128
    for index, s_ref in ((tp, so_ref), (1 - tp, st_ref)):
        for w in range(3):
            g = gq_ref[...] if w == 0 else low[:, (w - 1) * cols : w * cols]
            product = mm_tn(s_ref[...], g)
            for half in range(halves):
                at = pl.multiple_of((w * halves + half) * depth + index * width, 128)
                gw_ref[pl.ds(at, width), :] = product[:, half * 128 : (half + 1) * 128]


def reduce_kernel(
    bits,
    gw_ref,
    gow_ref,
    taps_ref,
    gqw_ref,
    gkw_ref,
    gvw_ref,
    go_ref,
    taps_out_ref,
    acc,
    outgoing,
    incoming,
    final,
    taps_in,
    taps_sum,
    s_send,
    s_recv,
    g_send,
    g_recv,
    t_send,
    t_recv,
):
    me = lax.axis_index("slab")
    count = len(bits)
    span = acc.shape[0] // 2
    orders = (bits, bits[:1] + bits[2:] + bits[1:2])

    def bit_of(b):
        return lax.rem(lax.div(me, 1 << b), 2)

    def partner(b):
        return me + (1 - 2 * bit_of(b)) * (1 << b)

    barrier = pltpu.get_barrier_semaphore()
    for b in bits:
        pl.semaphore_signal(
            barrier, inc=1, device_id={"slab": partner(b)}, device_id_type=MESH
        )
    gw_rows = gw_ref.shape[0]
    acc[0:gw_rows, :] = gw_ref[...]
    acc[gw_rows:, :] = gow_ref[...]
    taps_sum[0] = taps_ref[...]
    pl.semaphore_wait(barrier, count)

    lows = [jnp.int32(0), jnp.int32(span)]
    trail = [[], []]
    waits = []
    size = span
    offset = 0
    for k in range(count):
        size //= 2
        copies = []
        for t in range(2):
            b = orders[t][k]
            bit = bit_of(b)
            keep = lows[t] + bit * size
            give = lows[t] + (1 - bit) * size
            slots = pl.ds(offset, size)
            outgoing[t, slots, :] = acc[pl.ds(pl.multiple_of(give, 16), size), :].astype(BF16)
            copy = pltpu.make_async_remote_copy(
                src_ref=outgoing.at[t, slots],
                dst_ref=incoming.at[t, slots],
                send_sem=s_send.at[t, k],
                recv_sem=s_recv.at[t, k],
                device_id={"slab": partner(b)},
                device_id_type=MESH,
            )
            copy.start()
            copies.append(copy)
            lows[t] = keep
            trail[t].append(keep)
        b = orders[0][k]
        taps_copy = pltpu.make_async_remote_copy(
            src_ref=taps_sum.at[k],
            dst_ref=taps_in.at[k],
            send_sem=t_send.at[k],
            recv_sem=t_recv.at[k],
            device_id={"slab": partner(b)},
            device_id_type=MESH,
        )
        taps_copy.start()
        for t in range(2):
            copies[t].wait_recv()
            at = pl.ds(pl.multiple_of(lows[t], 16), size)
            acc[at, :] = acc[at, :] + incoming[t, pl.ds(offset, size), :].astype(F32)
        taps_copy.wait_recv()
        taps_sum[k + 1] = taps_sum[k] + taps_in[k]
        waits += copies + [taps_copy]
        offset += size
    for t in range(2):
        at = pl.ds(pl.multiple_of(lows[t], 16), size)
        final[at, :] = acc[at, :].astype(BF16)
    for k in range(count - 1, -1, -1):
        copies = []
        for t in range(2):
            at = pl.ds(pl.multiple_of(trail[t][k], 16), size)
            copy = pltpu.make_async_remote_copy(
                src_ref=final.at[at],
                dst_ref=final.at[at],
                send_sem=g_send.at[t, k],
                recv_sem=g_recv.at[t, k],
                device_id={"slab": partner(orders[t][k])},
                device_id_type=MESH,
            )
            copy.start()
            copies.append(copy)
        for copy in copies:
            copy.wait_recv()
        waits += copies
        size *= 2
    for copy in waits:
        copy.wait_send()
    depth, cols = gqw_ref.shape
    at = 0
    for out in (gqw_ref, gkw_ref, gvw_ref, go_ref):
        rows = out.shape[0]
        for half in range(out.shape[1] // 128):
            out[:, half * 128 : (half + 1) * 128] = final[at : at + rows, :].astype(F32)
            at += rows
    taps_out_ref[...] = taps_sum[count]


def reduce_all(gw, gow, taps, depth, cols, slabs):
    rows = gw.shape[0] + gow.shape[0]
    bits = tuple(range(slabs.bit_length() - 1))
    count = len(bits)
    shapes = [jax.ShapeDtypeStruct((depth, cols), F32)] * 3
    shapes.append(jax.ShapeDtypeStruct((cols, depth), F32))
    shapes.append(jax.ShapeDtypeStruct(taps.shape, F32))
    dma = pltpu.SemaphoreType.DMA
    return pl.pallas_call(
        functools.partial(reduce_kernel, bits),
        out_shape=shapes,
        in_specs=[VMEM] * 3,
        out_specs=[VMEM] * 5,
        scratch_shapes=[
            pltpu.VMEM((rows, 128), F32),
            pltpu.VMEM((2, rows // 2, 128), BF16),
            pltpu.VMEM((2, rows // 2, 128), BF16),
            pltpu.VMEM((rows, 128), BF16),
            pltpu.VMEM((count,) + taps.shape, F32),
            pltpu.VMEM((count + 1,) + taps.shape, F32),
            dma((2, count)),
            dma((2, count)),
            dma((2, count)),
            dma((2, count)),
            dma((count,)),
            dma((count,)),
        ],
        compiler_params=pltpu.CompilerParams(
            collective_id=0, has_side_effects=True, vmem_limit_bytes=LIMIT
        ),
    )(gw, gow, taps)


def body(
    slabs,
    tokens,
    stem_taps,
    query_weight,
    key_weight,
    value_weight,
    out_weight,
    key_blocks,
    counts,
    cotangent,
):
    count, width = tokens.shape
    depth, cols = query_weight.shape
    plane = PLANE_TOK
    sds = jax.ShapeDtypeStruct
    params = pltpu.CompilerParams(vmem_limit_bytes=LIMIT)
    up = [(i, (i + 1) % slabs) for i in range(slabs)]
    down = [(i, (i - 1) % slabs) for i in range(slabs)]

    def to_next(x):
        return lax.ppermute(x, "slab", up)

    def to_prev(x):
        return lax.ppermute(x, "slab", down)

    def swap(x):
        return lax.ppermute(x, "tp", [(0, 1), (1, 0)])

    before = jnp.concatenate([to_next(tokens[count - plane :]), tokens[: count - plane]])
    after = jnp.concatenate([tokens[plane:], to_prev(tokens[:plane])])
    before_f, own_f, after_f = before.astype(F32), tokens.astype(F32), after.astype(F32)
    stem = (stem_taps[0] * before_f + stem_taps[1] * own_f + stem_taps[2] * after_f).astype(BF16)
    stem_other = swap(stem)
    cot_other = swap(cotangent)

    q, kv = pl.pallas_call(
        project_kernel,
        out_shape=[sds((count, cols), BF16), sds((count, 2 * cols), BF16)],
        in_specs=[VMEM] * 5,
        out_specs=[VMEM] * 2,
        compiler_params=params,
    )(stem, stem_other, query_weight, key_weight, value_weight)
    kv_prev = to_next(kv[count - plane :])
    kv_next = to_prev(kv[:plane])

    gq, gkv, gprev, gnext, mix, mix_other, gow = pl.pallas_call(
        functools.partial(attention_kernel, slabs),
        out_shape=[
            sds((count, cols), BF16),
            sds((count, 2 * cols), F32),
            sds((plane, 2 * cols), BF16),
            sds((plane, 2 * cols), BF16),
            sds((count, width), F32),
            sds((count, width), BF16),
            sds((cols * depth // 128, 128), F32),
        ],
        in_specs=[SMEM, SMEM, VMEM, ANY, ANY, ANY, VMEM, VMEM, VMEM],
        out_specs=[VMEM] * 7,
        scratch_shapes=[
            pltpu.VMEM((count + 2 * plane, 2 * cols), BF16),
            pltpu.VMEM((count + 2 * plane, 2 * cols), F32),
            pltpu.VMEM((count, cols), BF16),
            pltpu.VMEM((count, cols), BF16),
            pltpu.SemaphoreType.DMA((3,)),
        ],
        compiler_params=params,
    )(key_blocks, counts, q, kv, kv_prev, kv_next, cotangent, cot_other, out_weight)
    from_next = to_prev(gprev)
    from_prev = to_next(gnext)
    layer_out = (stem.astype(F32) + (mix + swap(mix_other).astype(F32))).astype(BF16)

    own, other, gw = pl.pallas_call(
        gradient_kernel,
        out_shape=[
            sds((count, width), F32),
            sds((count, width), BF16),
            sds((3 * depth * cols // 128, 128), F32),
        ],
        in_specs=[VMEM] * 9,
        out_specs=[VMEM] * 3,
        scratch_shapes=[pltpu.VMEM((count, 2 * cols), BF16)],
        compiler_params=params,
    )(gq, gkv, from_prev, from_next, stem, stem_other, query_weight, key_weight, value_weight)

    grad_stem = cotangent.astype(F32) + (own + swap(other).astype(F32))
    grad_low = grad_stem.astype(BF16)
    grad_prev = to_next(grad_low[count - plane :]).astype(F32)
    grad_next = to_prev(grad_low[:plane]).astype(F32)
    grad_after = jnp.concatenate([grad_stem[plane:], grad_next])
    grad_before = jnp.concatenate([grad_prev, grad_stem[: count - plane]])
    grad_tokens = (
        stem_taps[0] * grad_after + stem_taps[1] * grad_stem + stem_taps[2] * grad_before
    )
    taps = jnp.stack([jnp.sum(grad_stem * x, axis=0) for x in (before_f, own_f, after_f)])
    gqw, gkw, gvw, go, grad_taps = reduce_all(gw, gow, taps, depth, cols, slabs)
    return (layer_out, grad_tokens, grad_taps, gqw, gkw, gvw, go)


def solution(mesh):
    in_specs = (
        P("slab", "tp"),
        P(None, "tp"),
        P(None, "tp"),
        P(None, "tp"),
        P(None, "tp"),
        P("tp", None),
        P("slab", None),
        P("slab"),
        P("slab", "tp"),
    )
    out_specs = (
        P("slab", "tp"),
        P("slab", "tp"),
        P(None, "tp"),
        P(None, "tp"),
        P(None, "tp"),
        P(None, "tp"),
        P("tp", None),
    )
    return jax.shard_map(
        functools.partial(body, mesh.shape["slab"]),
        mesh=mesh,
        in_specs=in_specs,
        out_specs=out_specs,
        check_vma=False,
    )
```

```python
import functools

import jax
import jax.numpy as jnp
from jax import lax
from jax.experimental import pallas as pl
from jax.experimental.pallas import tpu as pltpu
from jax.sharding import PartitionSpec as P

HD = 64
BLK = 128
PLANE_TOK = 512
MAXK = 4
NEG = -1e30
F32 = jnp.float32
BF16 = jnp.bfloat16
MESH = pl.DeviceIdType.MESH
VMEM = pl.BlockSpec(memory_space=pltpu.VMEM)
SMEM = pl.BlockSpec(memory_space=pltpu.SMEM)
ANY = pl.BlockSpec(memory_space=pl.ANY)
LIMIT = 60 * 1024 * 1024
CHUNK = 256


def mm(a, b):
    return jnp.dot(a, b, preferred_element_type=F32)


def mm_nt(a, b):
    return lax.dot_general(a, b, (((1,), (1,)), ((), ())), preferred_element_type=F32)


def mm_tn(a, b):
    return lax.dot_general(a, b, (((0,), (0,)), ((), ())), preferred_element_type=F32)


def part(index, width):
    return pl.ds(pl.multiple_of(index * width, width), width)


def project_kernel(so_ref, st_ref, wq_ref, wk_ref, wv_ref, q_ref, kv_ref):
    tp = lax.axis_index("tp")
    width = so_ref.shape[1]
    cols = wq_ref.shape[1]
    mine, other = part(tp, width), part(1 - tp, width)

    @pl.loop(0, so_ref.shape[0] // CHUNK)
    def _(step):
        rows = part(step, CHUNK)
        so, st = so_ref[rows, :], st_ref[rows, :]

        def project(w_ref):
            return (mm(so, w_ref[mine, :]) + mm(st, w_ref[other, :])).astype(BF16)

        q_ref[rows, :] = project(wq_ref)
        kv_ref[rows, 0:cols] = project(wk_ref)
        kv_ref[rows, cols : 2 * cols] = project(wv_ref)


def attention_kernel(
    slabs,
    blocks_ref,
    counts_ref,
    q_ref,
    kv_ref,
    kv_prev_ref,
    kv_next_ref,
    co_ref,
    ct_ref,
    ow_ref,
    gq_ref,
    gkv_ref,
    gprev_ref,
    gnext_ref,
    mix_ref,
    mix_other_ref,
    gow_ref,
    ext,
    acc,
    grad,
    attn,
    sems,
):
    tp = lax.axis_index("tp")
    slab = lax.axis_index("slab")
    tokens, cols = q_ref.shape
    width = co_ref.shape[1]
    heads = cols // HD
    planes = tokens // PLANE_TOK
    per_plane = PLANE_TOK // BLK
    total = planes * slabs
    copies = [
        pltpu.make_async_copy(kv_prev_ref, ext.at[0:PLANE_TOK], sems.at[0]),
        pltpu.make_async_copy(kv_ref, ext.at[PLANE_TOK : PLANE_TOK + tokens], sems.at[1]),
        pltpu.make_async_copy(
            kv_next_ref, ext.at[PLANE_TOK + tokens : 2 * PLANE_TOK + tokens], sems.at[2]
        ),
    ]
    for copy in copies:
        copy.start()
    mine, other = part(tp, width), part(1 - tp, width)

    @pl.loop(0, tokens // CHUNK)
    def _(step):
        rows = part(step, CHUNK)
        grad[rows, :] = (
            mm_nt(co_ref[rows, :], ow_ref[:, mine]) + mm_nt(ct_ref[rows, :], ow_ref[:, other])
        ).astype(BF16)

    @pl.loop(0, acc.shape[0] // BLK)
    def _(step):
        acc[part(step, BLK), :] = jnp.zeros((BLK, 2 * cols), F32)

    for copy in copies:
        copy.wait()

    lane = lax.broadcasted_iota(jnp.int32, (1, cols), 1) // HD
    masks = [(lane == h).astype(F32).astype(BF16) for h in range(heads)]
    slot = lax.broadcasted_iota(jnp.int32, (1, MAXK * BLK), 1)

    def stack(block):
        return jnp.concatenate([block * mask for mask in masks], axis=0)

    def pick(value):
        out = value[0:BLK]
        for h in range(1, heads):
            out = jnp.where(lane == h, value[h * BLK : (h + 1) * BLK], out)
        return out

    @pl.loop(0, tokens // BLK)
    def _(i):
        rows = part(i, BLK)
        where = []
        for j in range(MAXK):
            block = blocks_ref[i, j]
            plane = lax.rem(
                lax.div(block, per_plane) - slab * planes + 1 + total, total
            )
            where.append(part(plane * per_plane + lax.rem(block, per_plane), BLK))
        keys = jnp.concatenate([ext[at, 0:cols] for at in where], axis=0)
        values = jnp.concatenate([ext[at, cols : 2 * cols] for at in where], axis=0)
        queries = stack(q_ref[rows, :] * jnp.asarray(HD**-0.5, BF16))
        grads = stack(grad[rows, :])
        scores = mm_nt(queries, keys)
        scores = jnp.where(slot < counts_ref[i] * BLK, scores, NEG)
        exps = jnp.exp(scores - jnp.max(scores, axis=-1, keepdims=True))
        probs = exps * (1.0 / jnp.sum(exps, axis=-1, keepdims=True))
        low = probs.astype(BF16)
        attn[rows, :] = pick(mm(low, values)).astype(BF16)
        gprobs = mm_nt(grads, values)
        inner = jnp.sum(probs * gprobs, axis=-1, keepdims=True)
        gscores = (probs * (gprobs - inner)).astype(BF16)
        gq_ref[rows, :] = (pick(mm(gscores, keys)) * (HD**-0.5)).astype(BF16)
        gkeys = mm_tn(gscores, queries)
        gvalues = mm_tn(low, grads)
        for j in range(MAXK):
            acc[where[j], 0:cols] += gkeys[j * BLK : (j + 1) * BLK]
            acc[where[j], cols : 2 * cols] += gvalues[j * BLK : (j + 1) * BLK]

    gprev_ref[...] = acc[0:PLANE_TOK, :].astype(BF16)
    gkv_ref[...] = acc[PLANE_TOK : PLANE_TOK + tokens, :]
    gnext_ref[...] = acc[PLANE_TOK + tokens : 2 * PLANE_TOK + tokens, :].astype(BF16)

    @pl.loop(0, tokens // CHUNK)
    def _(step):
        rows = part(step, CHUNK)
        mix_ref[rows, :] = mm(attn[rows, :], ow_ref[:, mine])
        mix_other_ref[rows, :] = mm(attn[rows, :], ow_ref[:, other]).astype(BF16)

    halves = width // 128
    for index, c_ref in ((tp, co_ref), (1 - tp, ct_ref)):
        product = mm_tn(attn[...], c_ref[...])
        for half in range(halves):
            gow_ref[part(index * halves + half, cols), :] = product[
                :, half * 128 : (half + 1) * 128
            ]


def copy_to(src, dst, send, recv, where):
    return pltpu.make_async_remote_copy(
        src_ref=src,
        dst_ref=dst,
        send_sem=send,
        recv_sem=recv,
        device_id=where,
        device_id_type=MESH,
    )


def backward_kernel(
    slabs,
    gq_ref,
    gkv_ref,
    gprev_ref,
    gnext_ref,
    so_ref,
    st_ref,
    wq_ref,
    wk_ref,
    wv_ref,
    gow_ref,
    mix_ref,
    mix_other_ref,
    cot_ref,
    tok_ref,
    tok_prev_ref,
    tok_next_ref,
    taps_ref,
    layer_ref,
    grad_ref,
    final,
    taps_out_ref,
    low,
    from_prev,
    from_next,
    mix_in,
    own,
    other,
    part_out,
    part_in,
    edge,
    edge_prev,
    edge_next,
    acc,
    outgoing,
    incoming,
    taps_in,
    taps_sum,
    h_send,
    h_recv,
    m_send,
    m_recv,
    p_send,
    p_recv,
    e_send,
    e_recv,
    s_send,
    s_recv,
    t_send,
    t_recv,
):
    me = lax.axis_index("slab")
    tp = lax.axis_index("tp")
    bits = tuple(range(slabs.bit_length() - 1))
    stages = len(bits)
    orders = (bits, bits[:1] + bits[2:] + bits[1:2])
    tokens, cols = gq_ref.shape
    width = so_ref.shape[1]
    depth = wq_ref.shape[0]
    halves = cols // 128
    span = acc.shape[0] // 2
    last = tokens - PLANE_TOK
    chunks = tokens // CHUNK
    edge_chunks = PLANE_TOK // CHUNK
    mine, theirs = part(tp, width), part(1 - tp, width)
    nxt = {"slab": lax.rem(me + 1, slabs)}
    prv = {"slab": lax.rem(me + slabs - 1, slabs)}
    mate = {"tp": 1 - tp}

    def bit_of(b):
        return lax.rem(lax.div(me, 1 << b), 2)

    def partner(b):
        return {"slab": me + (1 - 2 * bit_of(b)) * (1 << b)}

    barrier = pltpu.get_barrier_semaphore()
    for where in [partner(b) for b in bits] + [nxt, prv, mate]:
        pl.semaphore_signal(barrier, inc=1, device_id=where, device_id_type=MESH)
    pl.semaphore_wait(barrier, stages + 3)

    down = copy_to(gprev_ref, from_next, h_send.at[0], h_recv.at[0], prv)
    up = copy_to(gnext_ref, from_prev, h_send.at[1], h_recv.at[1], nxt)
    mix_copy = copy_to(mix_other_ref, mix_in, m_send, m_recv, mate)
    down.start()
    up.start()
    mix_copy.start()
    sent = [down, up, mix_copy]

    lows = [jnp.int32(0), jnp.int32(span)]
    trail = [[], []]
    step_of = [0, 0]
    flight = [None, None]

    def rows_at(at, size):
        return pl.ds(pl.multiple_of(at, 16), size)

    def advance(t):
        k = step_of[t]
        if k > 2 * stages:
            return
        if flight[t] is not None:
            flight[t].wait_recv()
            sent.append(flight[t])
            if k <= stages:
                size = span >> k
                at = rows_at(lows[t], size)
                offset = span - 2 * size
                acc[at, :] = acc[at, :] + incoming[t, pl.ds(offset, size), :].astype(F32)
        if k == stages:
            at = rows_at(lows[t], span >> stages)
            final[at, :] = acc[at, :].astype(BF16)
        if k < stages:
            size = span >> (k + 1)
            b = orders[t][k]
            bit = bit_of(b)
            keep = lows[t] + bit * size
            give = lows[t] + (1 - bit) * size
            slots = pl.ds(span - 2 * size, size)
            outgoing[t, slots, :] = acc[rows_at(give, size), :].astype(BF16)
            flight[t] = copy_to(
                outgoing.at[t, slots],
                incoming.at[t, slots],
                s_send.at[t, k],
                s_recv.at[t, k],
                partner(b),
            )
            flight[t].start()
            lows[t] = keep
            trail[t].append(keep)
        elif k < 2 * stages:
            j = 2 * stages - 1 - k
            at = rows_at(trail[t][j], span >> (j + 1))
            flight[t] = copy_to(
                final.at[at],
                final.at[at],
                s_send.at[t, k],
                s_recv.at[t, k],
                partner(orders[t][j]),
            )
            flight[t].start()
        step_of[t] = k + 1

    def weight_gradient(base, g):
        for index, s_ref in ((tp, so_ref), (1 - tp, st_ref)):
            product = mm_tn(s_ref[...], g)
            for half in range(halves):
                at = pl.multiple_of(base + half * depth + index * width, 128)
                acc[pl.ds(at, width), :] = product[:, half * 128 : (half + 1) * 128]

    block = depth * halves
    weight_gradient(0, gq_ref[...])
    acc[block : 2 * block, :] = gow_ref[...]
    advance(0)
    for c in range(chunks):
        rows = slice(c * CHUNK, (c + 1) * CHUNK)
        gq = gq_ref[rows, :]
        own[rows, :] = mm_nt(gq, wq_ref[mine, :])
        other[rows, :] = mm_nt(gq, wq_ref[theirs, :])
    advance(0)
    down.wait_recv()
    up.wait_recv()
    parts = []
    for c in range(chunks):
        rows = slice(c * CHUNK, (c + 1) * CHUNK)
        total = gkv_ref[rows, :]
        if c < edge_chunks:
            total = total + from_prev[rows, :].astype(F32)
        if c >= chunks - edge_chunks:
            edge_rows = slice(c * CHUNK - last, (c + 1) * CHUNK - last)
            total = total + from_next[edge_rows, :].astype(F32)
        total = total.astype(BF16)
        low[rows, :] = total
        gk, gv = total[:, :cols], total[:, cols:]
        part_out[rows, :] = (
            other[rows, :] + mm_nt(gk, wk_ref[theirs, :]) + mm_nt(gv, wv_ref[theirs, :])
        ).astype(BF16)
        copy = copy_to(part_out.at[rows], part_in.at[rows], p_send.at[c], p_recv.at[c], mate)
        copy.start()
        parts.append(copy)
        own[rows, :] += mm_nt(gk, wk_ref[mine, :]) + mm_nt(gv, wv_ref[mine, :])
    advance(0)
    weight_gradient(2 * block, low[:, :cols])
    weight_gradient(3 * block, low[:, cols:])
    advance(1)
    advance(0)
    advance(1)
    mix_copy.wait_recv()
    layer_ref[...] = (
        so_ref[...].astype(F32) + (mix_ref[...] + mix_in[...].astype(F32))
    ).astype(BF16)
    advance(0)
    edges_low, edges_high = [], []
    for c in range(chunks):
        rows = slice(c * CHUNK, (c + 1) * CHUNK)
        parts[c].wait_recv()
        stem_grad = cot_ref[rows, :].astype(F32) + (own[rows, :] + part_in[rows, :].astype(F32))
        own[rows, :] = stem_grad
        edge[rows, :] = stem_grad.astype(BF16)
        if c < edge_chunks:
            copy = copy_to(
                edge.at[rows], edge_next.at[rows], e_send.at[0, c], e_recv.at[0, c], prv
            )
            copy.start()
            edges_low.append(copy)
        if c >= chunks - edge_chunks:
            e = c - (chunks - edge_chunks)
            edge_rows = slice(e * CHUNK, (e + 1) * CHUNK)
            copy = copy_to(
                edge.at[rows], edge_prev.at[edge_rows], e_send.at[1, e], e_recv.at[1, e], nxt
            )
            copy.start()
            edges_high.append(copy)
        if c % 2 == 0:
            advance(1)
    advance(0)
    sums = [jnp.zeros((1, width), F32) for _ in range(3)]
    for c in range(chunks):
        rows = slice(c * CHUNK, (c + 1) * CHUNK)
        g = own[rows, :]
        if c < edge_chunks:
            before = tok_prev_ref[rows, :]
        else:
            before = tok_ref[(c - edge_chunks) * CHUNK : (c - edge_chunks + 1) * CHUNK, :]
        if c >= chunks - edge_chunks:
            e = c - (chunks - edge_chunks)
            after = tok_next_ref[e * CHUNK : (e + 1) * CHUNK, :]
        else:
            after = tok_ref[(c + edge_chunks) * CHUNK : (c + edge_chunks + 1) * CHUNK, :]
        for n, x in enumerate((before, tok_ref[rows, :], after)):
            sums[n] = sums[n] + jnp.sum(g * x.astype(F32), axis=0, keepdims=True)
    taps_sum[0] = jnp.concatenate(sums + [jnp.zeros((5, width), F32)], axis=0)

    def send_taps(k):
        copy = copy_to(
            taps_sum.at[k], taps_in.at[k], t_send.at[k], t_recv.at[k], partner(bits[k])
        )
        copy.start()
        return copy

    def take_taps(k, copy):
        copy.wait_recv()
        sent.append(copy)
        taps_sum[k + 1] = taps_sum[k] + taps_in[k]

    def finish_tokens():
        for copy in edges_low + edges_high:
            copy.wait_recv()
        for c in range(chunks):
            rows = slice(c * CHUNK, (c + 1) * CHUNK)
            if c < edge_chunks:
                before = edge_prev[rows, :].astype(F32)
            else:
                before = own[(c - edge_chunks) * CHUNK : (c - edge_chunks + 1) * CHUNK, :]
            if c >= chunks - edge_chunks:
                e = c - (chunks - edge_chunks)
                after = edge_next[e * CHUNK : (e + 1) * CHUNK, :].astype(F32)
            else:
                after = own[(c + edge_chunks) * CHUNK : (c + edge_chunks + 1) * CHUNK, :]
            grad_ref[rows, :] = (
                taps_ref[0:1, :] * after + taps_ref[1:2, :] * own[rows, :]
                + taps_ref[2:3, :] * before
            )

    for k in range(stages):
        copy = send_taps(k)
        advance(1)
        advance(0)
        if k == 1:
            finish_tokens()
        take_taps(k, copy)
    if stages < 2:
        finish_tokens()
    for _ in range(2 * stages):
        advance(0)
        advance(1)
    taps_out_ref[...] = taps_sum[stages]
    for copy in sent + parts + edges_low + edges_high:
        copy.wait_send()


def unpack_kernel(final_ref, taps_in_ref, gqw_ref, gkw_ref, gvw_ref, go_ref, taps_ref):
    at = 0
    for out in (gqw_ref, go_ref, gkw_ref, gvw_ref):
        rows = out.shape[0]
        for half in range(out.shape[1] // 128):
            out[:, half * 128 : (half + 1) * 128] = final_ref[at : at + rows, :].astype(F32)
            at += rows
    taps_ref[...] = taps_in_ref[0:3, :]


def body(
    slabs,
    tokens,
    stem_taps,
    query_weight,
    key_weight,
    value_weight,
    out_weight,
    key_blocks,
    counts,
    cotangent,
):
    count, width = tokens.shape
    depth, cols = query_weight.shape
    plane = PLANE_TOK
    sds = jax.ShapeDtypeStruct
    params = pltpu.CompilerParams(vmem_limit_bytes=LIMIT)
    up = [(i, (i + 1) % slabs) for i in range(slabs)]
    down = [(i, (i - 1) % slabs) for i in range(slabs)]

    def to_next(x):
        return lax.ppermute(x, "slab", up)

    def to_prev(x):
        return lax.ppermute(x, "slab", down)

    def swap(x):
        return lax.ppermute(x, "tp", [(0, 1), (1, 0)])

    tok_prev = to_next(tokens[count - plane :])
    tok_next = to_prev(tokens[:plane])
    before = jnp.concatenate([tok_prev, tokens[: count - plane]])
    after = jnp.concatenate([tokens[plane:], tok_next])
    before_f, own_f, after_f = before.astype(F32), tokens.astype(F32), after.astype(F32)
    stem = (stem_taps[0] * before_f + stem_taps[1] * own_f + stem_taps[2] * after_f).astype(BF16)
    stem_other = swap(stem)
    cot_other = swap(cotangent)

    q, kv = pl.pallas_call(
        project_kernel,
        out_shape=[sds((count, cols), BF16), sds((count, 2 * cols), BF16)],
        in_specs=[VMEM] * 5,
        out_specs=[VMEM] * 2,
        compiler_params=params,
    )(stem, stem_other, query_weight, key_weight, value_weight)
    kv_prev = to_next(kv[count - plane :])
    kv_next = to_prev(kv[:plane])

    gq, gkv, gprev, gnext, mix, mix_other, gow = pl.pallas_call(
        functools.partial(attention_kernel, slabs),
        out_shape=[
            sds((count, cols), BF16),
            sds((count, 2 * cols), F32),
            sds((plane, 2 * cols), BF16),
            sds((plane, 2 * cols), BF16),
            sds((count, width), F32),
            sds((count, width), BF16),
            sds((cols * depth // 128, 128), F32),
        ],
        in_specs=[SMEM, SMEM, VMEM, ANY, ANY, ANY, VMEM, VMEM, VMEM],
        out_specs=[VMEM] * 7,
        scratch_shapes=[
            pltpu.VMEM((count + 2 * plane, 2 * cols), BF16),
            pltpu.VMEM((count + 2 * plane, 2 * cols), F32),
            pltpu.VMEM((count, cols), BF16),
            pltpu.VMEM((count, cols), BF16),
            pltpu.SemaphoreType.DMA((3,)),
        ],
        compiler_params=params,
    )(key_blocks, counts, q, kv, kv_prev, kv_next, cotangent, cot_other, out_weight)
    stages = slabs.bit_length() - 1
    chunks = count // CHUNK
    edge_chunks = plane // CHUNK
    rows = 4 * depth * cols // 128
    dma = pltpu.SemaphoreType.DMA
    layer_out, grad_tokens, final, taps = pl.pallas_call(
        functools.partial(backward_kernel, slabs),
        out_shape=[
            sds((count, width), BF16),
            sds((count, width), F32),
            sds((rows, 128), BF16),
            sds((8, width), F32),
        ],
        in_specs=[VMEM] * 17,
        out_specs=[VMEM] * 4,
        scratch_shapes=[
            pltpu.VMEM((count, 2 * cols), BF16),
            pltpu.VMEM((plane, 2 * cols), BF16),
            pltpu.VMEM((plane, 2 * cols), BF16),
            pltpu.VMEM((count, width), BF16),
            pltpu.VMEM((count, width), F32),
            pltpu.VMEM((count, width), F32),
            pltpu.VMEM((count, width), BF16),
            pltpu.VMEM((count, width), BF16),
            pltpu.VMEM((count, width), BF16),
            pltpu.VMEM((plane, width), BF16),
            pltpu.VMEM((plane, width), BF16),
            pltpu.VMEM((rows, 128), F32),
            pltpu.VMEM((2, rows // 2, 128), BF16),
            pltpu.VMEM((2, rows // 2, 128), BF16),
            pltpu.VMEM((stages, 8, width), F32),
            pltpu.VMEM((stages + 1, 8, width), F32),
            dma((2,)),
            dma((2,)),
            dma,
            dma,
            dma((chunks,)),
            dma((chunks,)),
            dma((2, edge_chunks)),
            dma((2, edge_chunks)),
            dma((2, 2 * stages)),
            dma((2, 2 * stages)),
            dma((stages,)),
            dma((stages,)),
        ],
        compiler_params=pltpu.CompilerParams(
            collective_id=1, has_side_effects=True, vmem_limit_bytes=LIMIT
        ),
    )(
        gq,
        gkv,
        gprev,
        gnext,
        stem,
        stem_other,
        query_weight,
        key_weight,
        value_weight,
        gow,
        mix,
        mix_other,
        cotangent,
        tokens,
        tok_prev,
        tok_next,
        stem_taps,
    )
    gqw, gkw, gvw, go, grad_taps = pl.pallas_call(
        unpack_kernel,
        out_shape=[sds((depth, cols), F32)] * 3
        + [sds((cols, depth), F32), sds(stem_taps.shape, F32)],
        in_specs=[VMEM] * 2,
        out_specs=[VMEM] * 5,
        compiler_params=params,
    )(final, taps)
    return (layer_out, grad_tokens, grad_taps, gqw, gkw, gvw, go)


def solution(mesh):
    in_specs = (
        P("slab", "tp"),
        P(None, "tp"),
        P(None, "tp"),
        P(None, "tp"),
        P(None, "tp"),
        P("tp", None),
        P("slab", None),
        P("slab"),
        P("slab", "tp"),
    )
    out_specs = (
        P("slab", "tp"),
        P("slab", "tp"),
        P(None, "tp"),
        P(None, "tp"),
        P(None, "tp"),
        P(None, "tp"),
        P("tp", None),
    )
    return jax.shard_map(
        functools.partial(body, mesh.shape["slab"]),
        mesh=mesh,
        in_specs=in_specs,
        out_specs=out_specs,
        check_vma=False,
    )
```

```python
import functools

import jax
import jax.numpy as jnp
from jax import lax
from jax.experimental import pallas as pl
from jax.experimental.pallas import tpu as pltpu
from jax.sharding import PartitionSpec as P

HD = 64
BLK = 128
PLANE_TOK = 512
MAXK = 4
NEG = -1e30
F32 = jnp.float32
BF16 = jnp.bfloat16
MESH = pl.DeviceIdType.MESH
VMEM = pl.BlockSpec(memory_space=pltpu.VMEM)
SMEM = pl.BlockSpec(memory_space=pltpu.SMEM)
LIMIT = 60 * 1024 * 1024
CHUNK = 256


def mm(a, b):
    return jnp.dot(a, b, preferred_element_type=F32)


def mm_nt(a, b):
    return lax.dot_general(a, b, (((1,), (1,)), ((), ())), preferred_element_type=F32)


def mm_tn(a, b):
    return lax.dot_general(a, b, (((0,), (0,)), ((), ())), preferred_element_type=F32)


def part(index, width):
    return pl.ds(pl.multiple_of(index * width, width), width)


def copy_to(src, dst, send, recv, where):
    return pltpu.make_async_remote_copy(
        src_ref=src,
        dst_ref=dst,
        send_sem=send,
        recv_sem=recv,
        device_id=where,
        device_id_type=MESH,
    )


def forward_kernel(
    slabs,
    tok_ref,
    taps_ref,
    wq_ref,
    wk_ref,
    wv_ref,
    ow_ref,
    cot_ref,
    so_ref,
    st_ref,
    ct_ref,
    prev_ref,
    next_ref,
    q_ref,
    ext_ref,
    grad_ref,
    t_send,
    t_recv,
    s_send,
    s_recv,
    c_send,
    c_recv,
    k_send,
    k_recv,
):
    me = lax.axis_index("slab")
    tp = lax.axis_index("tp")
    tokens, width = tok_ref.shape
    cols = wq_ref.shape[1]
    chunks = tokens // CHUNK
    edge_chunks = PLANE_TOK // CHUNK
    last = tokens - PLANE_TOK
    mine, theirs = part(tp, width), part(1 - tp, width)
    nxt = {"slab": lax.rem(me + 1, slabs)}
    prv = {"slab": lax.rem(me + slabs - 1, slabs)}
    mate = {"tp": 1 - tp}
    barrier = pltpu.get_barrier_semaphore()
    for where in (nxt, prv, mate):
        pl.semaphore_signal(barrier, inc=1, device_id=where, device_id_type=MESH)
    pl.semaphore_wait(barrier, 3)

    def rows_of(c):
        return slice(c * CHUNK, (c + 1) * CHUNK)

    halo = [[], []]
    for e in range(edge_chunks):
        rows = rows_of(e)
        high = slice(last + e * CHUNK, last + (e + 1) * CHUNK)
        up = copy_to(tok_ref.at[high], prev_ref.at[rows], t_send.at[0, e], t_recv.at[0, e], nxt)
        down = copy_to(tok_ref.at[rows], next_ref.at[rows], t_send.at[1, e], t_recv.at[1, e], prv)
        up.start()
        down.start()
        halo[0].append(up)
        halo[1].append(down)
    order = sorted(range(chunks), key=lambda c: (c % edge_chunks, c))
    cots = [
        copy_to(cot_ref.at[rows_of(c)], ct_ref.at[rows_of(c)], c_send.at[c], c_recv.at[c], mate)
        for c in range(chunks)
    ]
    early = chunks // 2
    for c in range(early):
        cots[c].start()
    stems = {}
    for c in order:
        rows = rows_of(c)
        if c < edge_chunks:
            halo[0][c].wait_recv()
            before = prev_ref[rows, :]
        else:
            before = tok_ref[rows_of(c - edge_chunks), :]
        if c >= chunks - edge_chunks:
            e = c - (chunks - edge_chunks)
            halo[1][e].wait_recv()
            after = next_ref[rows_of(e), :]
        else:
            after = tok_ref[rows_of(c + edge_chunks), :]
        so_ref[rows, :] = (
            taps_ref[0:1, :] * before.astype(F32)
            + taps_ref[1:2, :] * tok_ref[rows, :].astype(F32)
            + taps_ref[2:3, :] * after.astype(F32)
        ).astype(BF16)
        stems[c] = copy_to(so_ref.at[rows], st_ref.at[rows], s_send.at[c], s_recv.at[c], mate)
        stems[c].start()
    for c in range(early, chunks):
        cots[c].start()

    def output_gradient(c):
        rows = rows_of(c)
        cots[c].wait_recv()
        grad_ref[rows, :] = (
            mm_nt(cot_ref[rows, :], ow_ref[:, mine]) + mm_nt(ct_ref[rows, :], ow_ref[:, theirs])
        ).astype(BF16)

    for c in range(early):
        output_gradient(c)
    edges = []
    for c in order:
        rows = rows_of(c)
        stems[c].wait_recv()
        so, st = so_ref[rows, :], st_ref[rows, :]

        def project(w_ref):
            return (mm(so, w_ref[mine, :]) + mm(st, w_ref[theirs, :])).astype(BF16)

        place = slice(PLANE_TOK + c * CHUNK, PLANE_TOK + (c + 1) * CHUNK)
        ext_ref[place, 0:cols] = project(wk_ref)
        ext_ref[place, cols : 2 * cols] = project(wv_ref)
        if c < edge_chunks:
            at = PLANE_TOK + tokens + c * CHUNK
            copy = copy_to(
                ext_ref.at[place],
                ext_ref.at[at : at + CHUNK],
                k_send.at[0, c],
                k_recv.at[0, c],
                prv,
            )
            copy.start()
            edges.append(copy)
        if c >= chunks - edge_chunks:
            e = c - (chunks - edge_chunks)
            copy = copy_to(
                ext_ref.at[place],
                ext_ref.at[rows_of(e)],
                k_send.at[1, e],
                k_recv.at[1, e],
                nxt,
            )
            copy.start()
            edges.append(copy)
        q_ref[rows, :] = project(wq_ref)
    for c in range(early, chunks):
        output_gradient(c)
    for copy in edges:
        copy.wait_recv()
    for copy in halo[0] + halo[1] + cots + list(stems.values()) + edges:
        copy.wait_send()


def attention_kernel(
    slabs,
    blocks_ref,
    counts_ref,
    q_ref,
    ext,
    grad,
    co_ref,
    ct_ref,
    ow_ref,
    gq_ref,
    gkv_ref,
    gprev_ref,
    gnext_ref,
    mix_ref,
    mix_other_ref,
    gow_ref,
    acc,
    attn,
):
    tp = lax.axis_index("tp")
    slab = lax.axis_index("slab")
    tokens, cols = q_ref.shape
    width = co_ref.shape[1]
    heads = cols // HD
    planes = tokens // PLANE_TOK
    per_plane = PLANE_TOK // BLK
    total = planes * slabs
    mine, other = part(tp, width), part(1 - tp, width)

    @pl.loop(0, acc.shape[0] // BLK)
    def _(step):
        acc[part(step, BLK), :] = jnp.zeros((BLK, 2 * cols), F32)

    lane = lax.broadcasted_iota(jnp.int32, (1, cols), 1) // HD
    masks = [(lane == h).astype(F32).astype(BF16) for h in range(heads)]
    slot = lax.broadcasted_iota(jnp.int32, (1, MAXK * BLK), 1)

    def stack(block):
        return jnp.concatenate([block * mask for mask in masks], axis=0)

    def pick(value):
        out = value[0:BLK]
        for h in range(1, heads):
            out = jnp.where(lane == h, value[h * BLK : (h + 1) * BLK], out)
        return out

    @pl.loop(0, tokens // BLK)
    def _(i):
        rows = part(i, BLK)
        where = []
        for j in range(MAXK):
            block = blocks_ref[i, j]
            plane = lax.rem(
                lax.div(block, per_plane) - slab * planes + 1 + total, total
            )
            where.append(part(plane * per_plane + lax.rem(block, per_plane), BLK))
        keys = jnp.concatenate([ext[at, 0:cols] for at in where], axis=0)
        values = jnp.concatenate([ext[at, cols : 2 * cols] for at in where], axis=0)
        queries = stack(q_ref[rows, :] * jnp.asarray(HD**-0.5, BF16))
        grads = stack(grad[rows, :])
        scores = mm_nt(queries, keys)
        scores = jnp.where(slot < counts_ref[i] * BLK, scores, NEG)
        exps = jnp.exp(scores - jnp.max(scores, axis=-1, keepdims=True))
        probs = exps * (1.0 / jnp.sum(exps, axis=-1, keepdims=True))
        low = probs.astype(BF16)
        attn[rows, :] = pick(mm(low, values)).astype(BF16)
        gprobs = mm_nt(grads, values)
        inner = jnp.sum(probs * gprobs, axis=-1, keepdims=True)
        gscores = (probs * (gprobs - inner)).astype(BF16)
        gq_ref[rows, :] = (pick(mm(gscores, keys)) * (HD**-0.5)).astype(BF16)
        gkeys = mm_tn(gscores, queries)
        gvalues = mm_tn(low, grads)
        for j in range(MAXK):
            acc[where[j], 0:cols] += gkeys[j * BLK : (j + 1) * BLK]
            acc[where[j], cols : 2 * cols] += gvalues[j * BLK : (j + 1) * BLK]

    gprev_ref[...] = acc[0:PLANE_TOK, :].astype(BF16)
    gkv_ref[...] = acc[PLANE_TOK : PLANE_TOK + tokens, :]
    gnext_ref[...] = acc[PLANE_TOK + tokens : 2 * PLANE_TOK + tokens, :].astype(BF16)

    @pl.loop(0, tokens // CHUNK)
    def _(step):
        rows = part(step, CHUNK)
        mix_ref[rows, :] = mm(attn[rows, :], ow_ref[:, mine])
        mix_other_ref[rows, :] = mm(attn[rows, :], ow_ref[:, other]).astype(BF16)

    halves = width // 128
    for index, c_ref in ((tp, co_ref), (1 - tp, ct_ref)):
        product = mm_tn(attn[...], c_ref[...])
        for half in range(halves):
            gow_ref[part(index * halves + half, cols), :] = product[
                :, half * 128 : (half + 1) * 128
            ]


def backward_kernel(
    slabs,
    gq_ref,
    gkv_ref,
    gprev_ref,
    gnext_ref,
    so_ref,
    st_ref,
    wq_ref,
    wk_ref,
    wv_ref,
    gow_ref,
    mix_ref,
    mix_other_ref,
    cot_ref,
    tok_ref,
    tok_prev_ref,
    tok_next_ref,
    taps_ref,
    layer_ref,
    grad_ref,
    final,
    taps_out_ref,
    low,
    from_prev,
    from_next,
    mix_in,
    own,
    other,
    part_out,
    part_in,
    edge,
    edge_prev,
    edge_next,
    acc,
    outgoing,
    incoming,
    taps_in,
    taps_sum,
    h_send,
    h_recv,
    m_send,
    m_recv,
    p_send,
    p_recv,
    e_send,
    e_recv,
    s_send,
    s_recv,
    t_send,
    t_recv,
):
    me = lax.axis_index("slab")
    tp = lax.axis_index("tp")
    bits = tuple(range(slabs.bit_length() - 1))
    stages = len(bits)
    orders = (bits, bits[:1] + bits[2:] + bits[1:2])
    tokens, cols = gq_ref.shape
    width = so_ref.shape[1]
    depth = wq_ref.shape[0]
    halves = cols // 128
    span = acc.shape[0] // 2
    last = tokens - PLANE_TOK
    chunks = tokens // CHUNK
    edge_chunks = PLANE_TOK // CHUNK
    mine, theirs = part(tp, width), part(1 - tp, width)
    nxt = {"slab": lax.rem(me + 1, slabs)}
    prv = {"slab": lax.rem(me + slabs - 1, slabs)}
    mate = {"tp": 1 - tp}

    def bit_of(b):
        return lax.rem(lax.div(me, 1 << b), 2)

    def partner(b):
        return {"slab": me + (1 - 2 * bit_of(b)) * (1 << b)}

    barrier = pltpu.get_barrier_semaphore()
    for where in [partner(b) for b in bits] + [nxt, prv, mate]:
        pl.semaphore_signal(barrier, inc=1, device_id=where, device_id_type=MESH)
    pl.semaphore_wait(barrier, stages + 3)

    down = copy_to(gprev_ref, from_next, h_send.at[0], h_recv.at[0], prv)
    up = copy_to(gnext_ref, from_prev, h_send.at[1], h_recv.at[1], nxt)
    mix_copy = copy_to(mix_other_ref, mix_in, m_send, m_recv, mate)
    down.start()
    up.start()
    mix_copy.start()
    sent = [down, up, mix_copy]

    lows = [jnp.int32(0), jnp.int32(span)]
    trail = [[], []]
    step_of = [0, 0]
    flight = [None, None]

    def rows_at(at, size):
        return pl.ds(pl.multiple_of(at, 16), size)

    def advance(t):
        k = step_of[t]
        if k > 2 * stages:
            return
        if flight[t] is not None:
            flight[t].wait_recv()
            sent.append(flight[t])
            if k <= stages:
                size = span >> k
                at = rows_at(lows[t], size)
                offset = span - 2 * size
                acc[at, :] = acc[at, :] + incoming[t, pl.ds(offset, size), :].astype(F32)
        if k == stages:
            at = rows_at(lows[t], span >> stages)
            final[at, :] = acc[at, :].astype(BF16)
        if k < stages:
            size = span >> (k + 1)
            b = orders[t][k]
            bit = bit_of(b)
            keep = lows[t] + bit * size
            give = lows[t] + (1 - bit) * size
            slots = pl.ds(span - 2 * size, size)
            outgoing[t, slots, :] = acc[rows_at(give, size), :].astype(BF16)
            flight[t] = copy_to(
                outgoing.at[t, slots],
                incoming.at[t, slots],
                s_send.at[t, k],
                s_recv.at[t, k],
                partner(b),
            )
            flight[t].start()
            lows[t] = keep
            trail[t].append(keep)
        elif k < 2 * stages:
            j = 2 * stages - 1 - k
            at = rows_at(trail[t][j], span >> (j + 1))
            flight[t] = copy_to(
                final.at[at],
                final.at[at],
                s_send.at[t, k],
                s_recv.at[t, k],
                partner(orders[t][j]),
            )
            flight[t].start()
        step_of[t] = k + 1

    def weight_gradient(base, g):
        for index, s_ref in ((tp, so_ref), (1 - tp, st_ref)):
            product = mm_tn(s_ref[...], g)
            for half in range(halves):
                at = pl.multiple_of(base + half * depth + index * width, 128)
                acc[pl.ds(at, width), :] = product[:, half * 128 : (half + 1) * 128]

    block = depth * halves
    weight_gradient(0, gq_ref[...])
    acc[block : 2 * block, :] = gow_ref[...]
    advance(0)
    for c in range(chunks):
        rows = slice(c * CHUNK, (c + 1) * CHUNK)
        gq = gq_ref[rows, :]
        own[rows, :] = mm_nt(gq, wq_ref[mine, :])
        other[rows, :] = mm_nt(gq, wq_ref[theirs, :])
    advance(0)
    down.wait_recv()
    up.wait_recv()
    parts = []
    for c in range(chunks):
        rows = slice(c * CHUNK, (c + 1) * CHUNK)
        total = gkv_ref[rows, :]
        if c < edge_chunks:
            total = total + from_prev[rows, :].astype(F32)
        if c >= chunks - edge_chunks:
            edge_rows = slice(c * CHUNK - last, (c + 1) * CHUNK - last)
            total = total + from_next[edge_rows, :].astype(F32)
        total = total.astype(BF16)
        low[rows, :] = total
        gk, gv = total[:, :cols], total[:, cols:]
        part_out[rows, :] = (
            other[rows, :] + mm_nt(gk, wk_ref[theirs, :]) + mm_nt(gv, wv_ref[theirs, :])
        ).astype(BF16)
        copy = copy_to(part_out.at[rows], part_in.at[rows], p_send.at[c], p_recv.at[c], mate)
        copy.start()
        parts.append(copy)
        own[rows, :] += mm_nt(gk, wk_ref[mine, :]) + mm_nt(gv, wv_ref[mine, :])
    advance(0)
    weight_gradient(2 * block, low[:, :cols])
    weight_gradient(3 * block, low[:, cols:])
    advance(1)
    advance(0)
    advance(1)
    mix_copy.wait_recv()
    layer_ref[...] = (
        so_ref[...].astype(F32) + (mix_ref[...] + mix_in[...].astype(F32))
    ).astype(BF16)
    advance(0)
    edges_low, edges_high = [], []
    for c in range(chunks):
        rows = slice(c * CHUNK, (c + 1) * CHUNK)
        parts[c].wait_recv()
        stem_grad = cot_ref[rows, :].astype(F32) + (own[rows, :] + part_in[rows, :].astype(F32))
        own[rows, :] = stem_grad
        edge[rows, :] = stem_grad.astype(BF16)
        if c < edge_chunks:
            copy = copy_to(
                edge.at[rows], edge_next.at[rows], e_send.at[0, c], e_recv.at[0, c], prv
            )
            copy.start()
            edges_low.append(copy)
        if c >= chunks - edge_chunks:
            e = c - (chunks - edge_chunks)
            edge_rows = slice(e * CHUNK, (e + 1) * CHUNK)
            copy = copy_to(
                edge.at[rows], edge_prev.at[edge_rows], e_send.at[1, e], e_recv.at[1, e], nxt
            )
            copy.start()
            edges_high.append(copy)
        if c % 2 == 0:
            advance(1)
    advance(0)
    sums = [jnp.zeros((1, width), F32) for _ in range(3)]
    for c in range(chunks):
        rows = slice(c * CHUNK, (c + 1) * CHUNK)
        g = own[rows, :]
        if c < edge_chunks:
            before = tok_prev_ref[rows, :]
        else:
            before = tok_ref[(c - edge_chunks) * CHUNK : (c - edge_chunks + 1) * CHUNK, :]
        if c >= chunks - edge_chunks:
            e = c - (chunks - edge_chunks)
            after = tok_next_ref[e * CHUNK : (e + 1) * CHUNK, :]
        else:
            after = tok_ref[(c + edge_chunks) * CHUNK : (c + edge_chunks + 1) * CHUNK, :]
        for n, x in enumerate((before, tok_ref[rows, :], after)):
            sums[n] = sums[n] + jnp.sum(g * x.astype(F32), axis=0, keepdims=True)
    taps_sum[0] = jnp.concatenate(sums + [jnp.zeros((5, width), F32)], axis=0)

    def send_taps(k):
        copy = copy_to(
            taps_sum.at[k], taps_in.at[k], t_send.at[k], t_recv.at[k], partner(bits[k])
        )
        copy.start()
        return copy

    def take_taps(k, copy):
        copy.wait_recv()
        sent.append(copy)
        taps_sum[k + 1] = taps_sum[k] + taps_in[k]

    def finish_tokens():
        for copy in edges_low + edges_high:
            copy.wait_recv()
        for c in range(chunks):
            rows = slice(c * CHUNK, (c + 1) * CHUNK)
            if c < edge_chunks:
                before = edge_prev[rows, :].astype(F32)
            else:
                before = own[(c - edge_chunks) * CHUNK : (c - edge_chunks + 1) * CHUNK, :]
            if c >= chunks - edge_chunks:
                e = c - (chunks - edge_chunks)
                after = edge_next[e * CHUNK : (e + 1) * CHUNK, :].astype(F32)
            else:
                after = own[(c + edge_chunks) * CHUNK : (c + edge_chunks + 1) * CHUNK, :]
            grad_ref[rows, :] = (
                taps_ref[0:1, :] * after + taps_ref[1:2, :] * own[rows, :]
                + taps_ref[2:3, :] * before
            )

    for k in range(stages):
        copy = send_taps(k)
        advance(1)
        advance(0)
        if k == 1:
            finish_tokens()
        take_taps(k, copy)
    if stages < 2:
        finish_tokens()
    for _ in range(2 * stages):
        advance(0)
        advance(1)
    taps_out_ref[...] = taps_sum[stages]
    for copy in sent + parts + edges_low + edges_high:
        copy.wait_send()


def unpack_kernel(final_ref, taps_in_ref, gqw_ref, gkw_ref, gvw_ref, go_ref, taps_ref):
    at = 0
    for out in (gqw_ref, go_ref, gkw_ref, gvw_ref):
        rows = out.shape[0]
        for half in range(out.shape[1] // 128):
            out[:, half * 128 : (half + 1) * 128] = final_ref[at : at + rows, :].astype(F32)
            at += rows
    taps_ref[...] = taps_in_ref[0:3, :]


def body(
    slabs,
    tokens,
    stem_taps,
    query_weight,
    key_weight,
    value_weight,
    out_weight,
    key_blocks,
    counts,
    cotangent,
):
    count, width = tokens.shape
    depth, cols = query_weight.shape
    plane = PLANE_TOK
    sds = jax.ShapeDtypeStruct
    params = pltpu.CompilerParams(vmem_limit_bytes=LIMIT)
    stages = slabs.bit_length() - 1
    chunks = count // CHUNK
    edge_chunks = plane // CHUNK
    dma = pltpu.SemaphoreType.DMA
    pairs = [(2, edge_chunks)] * 2 + [(chunks,)] * 4 + [(2, edge_chunks)] * 2
    stem, stem_other, cot_other, tok_prev, tok_next, q, ext, grad = pl.pallas_call(
        functools.partial(forward_kernel, slabs),
        out_shape=[
            sds((count, width), BF16),
            sds((count, width), BF16),
            sds((count, width), BF16),
            sds((plane, width), BF16),
            sds((plane, width), BF16),
            sds((count, cols), BF16),
            sds((count + 2 * plane, 2 * cols), BF16),
            sds((count, cols), BF16),
        ],
        in_specs=[VMEM] * 7,
        out_specs=[VMEM] * 8,
        scratch_shapes=[dma(shape) for shape in pairs],
        compiler_params=pltpu.CompilerParams(
            collective_id=0, has_side_effects=True, vmem_limit_bytes=LIMIT
        ),
    )(tokens, stem_taps, query_weight, key_weight, value_weight, out_weight, cotangent)

    gq, gkv, gprev, gnext, mix, mix_other, gow = pl.pallas_call(
        functools.partial(attention_kernel, slabs),
        out_shape=[
            sds((count, cols), BF16),
            sds((count, 2 * cols), F32),
            sds((plane, 2 * cols), BF16),
            sds((plane, 2 * cols), BF16),
            sds((count, width), F32),
            sds((count, width), BF16),
            sds((cols * depth // 128, 128), F32),
        ],
        in_specs=[SMEM, SMEM] + [VMEM] * 6,
        out_specs=[VMEM] * 7,
        scratch_shapes=[
            pltpu.VMEM((count + 2 * plane, 2 * cols), F32),
            pltpu.VMEM((count, cols), BF16),
        ],
        compiler_params=params,
    )(key_blocks, counts, q, ext, grad, cotangent, cot_other, out_weight)
    rows = 4 * depth * cols // 128
    layer_out, grad_tokens, final, taps = pl.pallas_call(
        functools.partial(backward_kernel, slabs),
        out_shape=[
            sds((count, width), BF16),
            sds((count, width), F32),
            sds((rows, 128), BF16),
            sds((8, width), F32),
        ],
        in_specs=[VMEM] * 17,
        out_specs=[VMEM] * 4,
        scratch_shapes=[
            pltpu.VMEM((count, 2 * cols), BF16),
            pltpu.VMEM((plane, 2 * cols), BF16),
            pltpu.VMEM((plane, 2 * cols), BF16),
            pltpu.VMEM((count, width), BF16),
            pltpu.VMEM((count, width), F32),
            pltpu.VMEM((count, width), F32),
            pltpu.VMEM((count, width), BF16),
            pltpu.VMEM((count, width), BF16),
            pltpu.VMEM((count, width), BF16),
            pltpu.VMEM((plane, width), BF16),
            pltpu.VMEM((plane, width), BF16),
            pltpu.VMEM((rows, 128), F32),
            pltpu.VMEM((2, rows // 2, 128), BF16),
            pltpu.VMEM((2, rows // 2, 128), BF16),
            pltpu.VMEM((stages, 8, width), F32),
            pltpu.VMEM((stages + 1, 8, width), F32),
            dma((2,)),
            dma((2,)),
            dma,
            dma,
            dma((chunks,)),
            dma((chunks,)),
            dma((2, edge_chunks)),
            dma((2, edge_chunks)),
            dma((2, 2 * stages)),
            dma((2, 2 * stages)),
            dma((stages,)),
            dma((stages,)),
        ],
        compiler_params=pltpu.CompilerParams(
            collective_id=1, has_side_effects=True, vmem_limit_bytes=LIMIT
        ),
    )(
        gq,
        gkv,
        gprev,
        gnext,
        stem,
        stem_other,
        query_weight,
        key_weight,
        value_weight,
        gow,
        mix,
        mix_other,
        cotangent,
        tokens,
        tok_prev,
        tok_next,
        stem_taps,
    )
    gqw, gkw, gvw, go, grad_taps = pl.pallas_call(
        unpack_kernel,
        out_shape=[sds((depth, cols), F32)] * 3
        + [sds((cols, depth), F32), sds(stem_taps.shape, F32)],
        in_specs=[VMEM] * 2,
        out_specs=[VMEM] * 5,
        compiler_params=params,
    )(final, taps)
    return (layer_out, grad_tokens, grad_taps, gqw, gkw, gvw, go)


def solution(mesh):
    in_specs = (
        P("slab", "tp"),
        P(None, "tp"),
        P(None, "tp"),
        P(None, "tp"),
        P(None, "tp"),
        P("tp", None),
        P("slab", None),
        P("slab"),
        P("slab", "tp"),
    )
    out_specs = (
        P("slab", "tp"),
        P("slab", "tp"),
        P(None, "tp"),
        P(None, "tp"),
        P(None, "tp"),
        P(None, "tp"),
        P("tp", None),
    )
    return jax.shard_map(
        functools.partial(body, mesh.shape["slab"]),
        mesh=mesh,
        in_specs=in_specs,
        out_specs=out_specs,
        check_vma=False,
    )
```

```python
import functools

import jax
import jax.numpy as jnp
from jax import lax
from jax.experimental import pallas as pl
from jax.experimental.pallas import tpu as pltpu
from jax.sharding import PartitionSpec as P

HD = 64
BLK = 128
PLANE_TOK = 512
MAXK = 4
NEG = -1e30
F32 = jnp.float32
BF16 = jnp.bfloat16
MESH = pl.DeviceIdType.MESH
VMEM = pl.BlockSpec(memory_space=pltpu.VMEM)
SMEM = pl.BlockSpec(memory_space=pltpu.SMEM)
MIB = 1024 * 1024
CHUNK = 256


def mm(a, b):
    return jnp.dot(a, b, preferred_element_type=F32)


def mm_nt(a, b):
    return lax.dot_general(a, b, (((1,), (1,)), ((), ())), preferred_element_type=F32)


def mm_tn(a, b):
    return lax.dot_general(a, b, (((0,), (0,)), ((), ())), preferred_element_type=F32)


def part(index, width):
    return pl.ds(pl.multiple_of(index * width, width), width)


def copy_to(src, dst, send, recv, where):
    return pltpu.make_async_remote_copy(
        src_ref=src,
        dst_ref=dst,
        send_sem=send,
        recv_sem=recv,
        device_id=where,
        device_id_type=MESH,
    )


def forward_kernel(
    slabs,
    tok_ref,
    taps_ref,
    wq_ref,
    wk_ref,
    wv_ref,
    ow_ref,
    cot_ref,
    so_ref,
    st_ref,
    ct_ref,
    prev_ref,
    next_ref,
    q_ref,
    ext_ref,
    grad_ref,
    t_send,
    t_recv,
    s_send,
    s_recv,
    c_send,
    c_recv,
    k_send,
    k_recv,
):
    me = lax.axis_index("slab")
    tp = lax.axis_index("tp")
    tokens, width = tok_ref.shape
    cols = wq_ref.shape[1]
    chunks = tokens // CHUNK
    edge_chunks = PLANE_TOK // CHUNK
    last = tokens - PLANE_TOK
    mine, theirs = part(tp, width), part(1 - tp, width)
    nxt = {"slab": lax.rem(me + 1, slabs)}
    prv = {"slab": lax.rem(me + slabs - 1, slabs)}
    mate = {"tp": 1 - tp}
    barrier = pltpu.get_barrier_semaphore()
    for where in (nxt, prv, mate):
        pl.semaphore_signal(barrier, inc=1, device_id=where, device_id_type=MESH)
    pl.semaphore_wait(barrier, 3)

    def rows_of(c):
        return slice(c * CHUNK, (c + 1) * CHUNK)

    halo = [[], []]
    for e in range(edge_chunks):
        rows = rows_of(e)
        high = slice(last + e * CHUNK, last + (e + 1) * CHUNK)
        up = copy_to(tok_ref.at[high], prev_ref.at[rows], t_send.at[0, e], t_recv.at[0, e], nxt)
        down = copy_to(tok_ref.at[rows], next_ref.at[rows], t_send.at[1, e], t_recv.at[1, e], prv)
        up.start()
        down.start()
        halo[0].append(up)
        halo[1].append(down)
    order = sorted(range(chunks), key=lambda c: (c % edge_chunks, c))
    cots = [
        copy_to(cot_ref.at[rows_of(c)], ct_ref.at[rows_of(c)], c_send.at[c], c_recv.at[c], mate)
        for c in range(chunks)
    ]
    early = chunks // 2
    for c in range(early):
        cots[c].start()
    stems = {}
    for c in order:
        rows = rows_of(c)
        if c < edge_chunks:
            halo[0][c].wait_recv()
            before = prev_ref[rows, :]
        else:
            before = tok_ref[rows_of(c - edge_chunks), :]
        if c >= chunks - edge_chunks:
            e = c - (chunks - edge_chunks)
            halo[1][e].wait_recv()
            after = next_ref[rows_of(e), :]
        else:
            after = tok_ref[rows_of(c + edge_chunks), :]
        so_ref[rows, :] = (
            taps_ref[0:1, :] * before.astype(F32)
            + taps_ref[1:2, :] * tok_ref[rows, :].astype(F32)
            + taps_ref[2:3, :] * after.astype(F32)
        ).astype(BF16)
        stems[c] = copy_to(so_ref.at[rows], st_ref.at[rows], s_send.at[c], s_recv.at[c], mate)
        stems[c].start()
    for c in range(early, chunks):
        cots[c].start()

    def output_gradient(c):
        rows = rows_of(c)
        cots[c].wait_recv()
        grad_ref[rows, :] = (
            mm_nt(cot_ref[rows, :], ow_ref[:, mine]) + mm_nt(ct_ref[rows, :], ow_ref[:, theirs])
        ).astype(BF16)

    for c in range(early):
        output_gradient(c)
    edges = []
    for c in order:
        rows = rows_of(c)
        stems[c].wait_recv()
        so, st = so_ref[rows, :], st_ref[rows, :]

        def project(w_ref):
            return (mm(so, w_ref[mine, :]) + mm(st, w_ref[theirs, :])).astype(BF16)

        place = slice(PLANE_TOK + c * CHUNK, PLANE_TOK + (c + 1) * CHUNK)
        ext_ref[place, 0:cols] = project(wk_ref)
        ext_ref[place, cols : 2 * cols] = project(wv_ref)
        if c < edge_chunks:
            at = PLANE_TOK + tokens + c * CHUNK
            copy = copy_to(
                ext_ref.at[place],
                ext_ref.at[at : at + CHUNK],
                k_send.at[0, c],
                k_recv.at[0, c],
                prv,
            )
            copy.start()
            edges.append(copy)
        if c >= chunks - edge_chunks:
            e = c - (chunks - edge_chunks)
            copy = copy_to(
                ext_ref.at[place],
                ext_ref.at[rows_of(e)],
                k_send.at[1, e],
                k_recv.at[1, e],
                nxt,
            )
            copy.start()
            edges.append(copy)
        q_ref[rows, :] = project(wq_ref)
    for c in range(early, chunks):
        output_gradient(c)
    for copy in edges:
        copy.wait_recv()
    for copy in halo[0] + halo[1] + cots + list(stems.values()) + edges:
        copy.wait_send()


def attention_kernel(
    slabs,
    blocks_ref,
    counts_ref,
    q_ref,
    ext,
    grad,
    co_ref,
    ct_ref,
    ow_ref,
    gq_ref,
    gkv_ref,
    gprev_ref,
    gnext_ref,
    mix_ref,
    mix_other_ref,
    gow_ref,
    acc,
    attn,
):
    tp = lax.axis_index("tp")
    slab = lax.axis_index("slab")
    tokens, cols = q_ref.shape
    width = co_ref.shape[1]
    heads = cols // HD
    planes = tokens // PLANE_TOK
    per_plane = PLANE_TOK // BLK
    total = planes * slabs
    mine, other = part(tp, width), part(1 - tp, width)

    @pl.loop(0, acc.shape[0] // BLK)
    def _(step):
        acc[part(step, BLK), :] = jnp.zeros((BLK, 2 * cols), F32)

    lane = lax.broadcasted_iota(jnp.int32, (1, cols), 1) // HD
    masks = [(lane == h).astype(F32).astype(BF16) for h in range(heads)]

    def stack(block):
        return jnp.concatenate([block * mask for mask in masks], axis=0)

    def pick(value):
        heads_t = [
            value[h * HD : (h + 1) * HD, h * BLK : (h + 1) * BLK] for h in range(heads)
        ]
        return jnp.concatenate(heads_t, axis=0).T

    @pl.loop(0, tokens // BLK)
    def _(i):
        rows = part(i, BLK)
        where = []
        for j in range(MAXK):
            block = blocks_ref[j, i]
            plane = lax.rem(
                lax.div(block, per_plane) - slab * planes + 1 + total, total
            )
            where.append(part(plane * per_plane + lax.rem(block, per_plane), BLK))
        keys = jnp.concatenate([ext[at, 0:cols] for at in where], axis=0)
        values = jnp.concatenate([ext[at, cols : 2 * cols] for at in where], axis=0)
        queries = stack(q_ref[rows, :] * jnp.asarray(HD**-0.5, BF16))
        grads = stack(grad[rows, :])
        scores = mm_nt(keys, queries)
        live = counts_ref[i]
        scores = jnp.concatenate(
            [
                jnp.where(j < live, scores[j * BLK : (j + 1) * BLK], NEG)
                for j in range(MAXK)
            ],
            axis=0,
        )
        exps = jnp.exp(scores - jnp.max(scores, axis=0, keepdims=True))
        probs = exps * (1.0 / jnp.sum(exps, axis=0, keepdims=True))
        low = probs.astype(BF16)
        attn[rows, :] = pick(mm_tn(values, low)).astype(BF16)
        gprobs = mm_nt(values, grads)
        inner = jnp.sum(probs * gprobs, axis=0, keepdims=True)
        gscores = (probs * (gprobs - inner)).astype(BF16)
        gq_ref[rows, :] = (pick(mm_tn(keys, gscores)) * (HD**-0.5)).astype(BF16)
        gkeys = mm(gscores, queries)
        gvalues = mm(low, grads)
        for j in range(MAXK):
            acc[where[j], 0:cols] += gkeys[j * BLK : (j + 1) * BLK]
            acc[where[j], cols : 2 * cols] += gvalues[j * BLK : (j + 1) * BLK]

    gprev_ref[...] = acc[0:PLANE_TOK, :].astype(BF16)
    gkv_ref[...] = acc[PLANE_TOK : PLANE_TOK + tokens, :]
    gnext_ref[...] = acc[PLANE_TOK + tokens : 2 * PLANE_TOK + tokens, :].astype(BF16)

    @pl.loop(0, tokens // CHUNK)
    def _(step):
        rows = part(step, CHUNK)
        mix_ref[rows, :] = mm(attn[rows, :], ow_ref[:, mine])
        mix_other_ref[rows, :] = mm(attn[rows, :], ow_ref[:, other]).astype(BF16)

    halves = width // 128
    for index, c_ref in ((tp, co_ref), (1 - tp, ct_ref)):
        product = mm_tn(attn[...], c_ref[...])
        for half in range(halves):
            gow_ref[part(index * halves + half, cols), :] = product[
                :, half * 128 : (half + 1) * 128
            ]


def backward_kernel(
    slabs,
    gq_ref,
    gkv_ref,
    gprev_ref,
    gnext_ref,
    so_ref,
    st_ref,
    wq_ref,
    wk_ref,
    wv_ref,
    gow_ref,
    mix_ref,
    mix_other_ref,
    cot_ref,
    tok_ref,
    tok_prev_ref,
    tok_next_ref,
    taps_ref,
    layer_ref,
    grad_ref,
    final,
    taps_out_ref,
    low,
    from_prev,
    from_next,
    mix_in,
    own,
    other,
    part_out,
    part_in,
    edge,
    edge_prev,
    edge_next,
    acc,
    outgoing,
    incoming,
    taps_in,
    taps_sum,
    h_send,
    h_recv,
    m_send,
    m_recv,
    p_send,
    p_recv,
    e_send,
    e_recv,
    s_send,
    s_recv,
    t_send,
    t_recv,
):
    me = lax.axis_index("slab")
    tp = lax.axis_index("tp")
    bits = tuple(range(slabs.bit_length() - 1))
    stages = len(bits)
    orders = (bits[:1] + bits[2:] + bits[1:2], bits)
    tokens, cols = gq_ref.shape
    width = so_ref.shape[1]
    depth = wq_ref.shape[0]
    halves = cols // 128
    span = acc.shape[0] // 2
    last = tokens - PLANE_TOK
    chunks = tokens // CHUNK
    edge_chunks = PLANE_TOK // CHUNK
    mine, theirs = part(tp, width), part(1 - tp, width)
    nxt = {"slab": lax.rem(me + 1, slabs)}
    prv = {"slab": lax.rem(me + slabs - 1, slabs)}
    mate = {"tp": 1 - tp}

    def bit_of(b):
        return lax.rem(lax.div(me, 1 << b), 2)

    def partner(b):
        return {"slab": me + (1 - 2 * bit_of(b)) * (1 << b)}

    barrier = pltpu.get_barrier_semaphore()
    for where in [partner(b) for b in bits] + [nxt, prv, mate]:
        pl.semaphore_signal(barrier, inc=1, device_id=where, device_id_type=MESH)
    pl.semaphore_wait(barrier, stages + 3)

    down = copy_to(gprev_ref, from_next, h_send.at[0], h_recv.at[0], prv)
    up = copy_to(gnext_ref, from_prev, h_send.at[1], h_recv.at[1], nxt)
    mix_copy = copy_to(mix_other_ref, mix_in, m_send, m_recv, mate)
    down.start()
    up.start()
    mix_copy.start()
    sent = [down, up, mix_copy]

    lows = [jnp.int32(0), jnp.int32(span)]
    trail = [[], []]
    step_of = [0, 0]
    flight = [None, None]

    def rows_at(at, size):
        return pl.ds(pl.multiple_of(at, 16), size)

    def advance(t):
        k = step_of[t]
        if k > 2 * stages:
            return
        if flight[t] is not None:
            flight[t].wait_recv()
            sent.append(flight[t])
            if k <= stages:
                size = span >> k
                at = rows_at(lows[t], size)
                offset = span - 2 * size
                acc[at, :] = acc[at, :] + incoming[t, pl.ds(offset, size), :].astype(F32)
        if k == stages:
            at = rows_at(lows[t], span >> stages)
            final[at, :] = acc[at, :].astype(BF16)
        if k < stages:
            size = span >> (k + 1)
            b = orders[t][k]
            bit = bit_of(b)
            keep = lows[t] + bit * size
            give = lows[t] + (1 - bit) * size
            slots = pl.ds(span - 2 * size, size)
            outgoing[t, slots, :] = acc[rows_at(give, size), :].astype(BF16)
            flight[t] = copy_to(
                outgoing.at[t, slots],
                incoming.at[t, slots],
                s_send.at[t, k],
                s_recv.at[t, k],
                partner(b),
            )
            flight[t].start()
            lows[t] = keep
            trail[t].append(keep)
        elif k < 2 * stages:
            j = 2 * stages - 1 - k
            at = rows_at(trail[t][j], span >> (j + 1))
            flight[t] = copy_to(
                final.at[at],
                final.at[at],
                s_send.at[t, k],
                s_recv.at[t, k],
                partner(orders[t][j]),
            )
            flight[t].start()
        step_of[t] = k + 1

    def weight_gradient(base, g):
        for index, s_ref in ((tp, so_ref), (1 - tp, st_ref)):
            product = mm_tn(s_ref[...], g)
            for half in range(halves):
                at = pl.multiple_of(base + half * depth + index * width, 128)
                acc[pl.ds(at, width), :] = product[:, half * 128 : (half + 1) * 128]

    block = depth * halves
    weight_gradient(0, gq_ref[...])
    acc[block : 2 * block, :] = gow_ref[...]
    advance(0)
    for c in range(chunks):
        rows = slice(c * CHUNK, (c + 1) * CHUNK)
        gq = gq_ref[rows, :]
        own[rows, :] = mm_nt(gq, wq_ref[mine, :])
        other[rows, :] = mm_nt(gq, wq_ref[theirs, :])
    advance(0)
    advance(0)
    down.wait_recv()
    up.wait_recv()
    parts = []
    for c in range(chunks):
        rows = slice(c * CHUNK, (c + 1) * CHUNK)
        total = gkv_ref[rows, :]
        if c < edge_chunks:
            total = total + from_prev[rows, :].astype(F32)
        if c >= chunks - edge_chunks:
            edge_rows = slice(c * CHUNK - last, (c + 1) * CHUNK - last)
            total = total + from_next[edge_rows, :].astype(F32)
        total = total.astype(BF16)
        low[rows, :] = total
        gk, gv = total[:, :cols], total[:, cols:]
        part_out[rows, :] = (
            other[rows, :] + mm_nt(gk, wk_ref[theirs, :]) + mm_nt(gv, wv_ref[theirs, :])
        ).astype(BF16)
        copy = copy_to(part_out.at[rows], part_in.at[rows], p_send.at[c], p_recv.at[c], mate)
        copy.start()
        parts.append(copy)
        own[rows, :] += mm_nt(gk, wk_ref[mine, :]) + mm_nt(gv, wv_ref[mine, :])
    advance(0)
    weight_gradient(2 * block, low[:, :cols])
    weight_gradient(3 * block, low[:, cols:])
    advance(1)
    advance(0)
    advance(1)
    mix_copy.wait_recv()
    layer_ref[...] = (
        so_ref[...].astype(F32) + (mix_ref[...] + mix_in[...].astype(F32))
    ).astype(BF16)
    advance(0)
    edges_low, edges_high = [], []
    for c in range(chunks):
        rows = slice(c * CHUNK, (c + 1) * CHUNK)
        parts[c].wait_recv()
        stem_grad = cot_ref[rows, :].astype(F32) + (own[rows, :] + part_in[rows, :].astype(F32))
        own[rows, :] = stem_grad
        edge[rows, :] = stem_grad.astype(BF16)
        if c < edge_chunks:
            copy = copy_to(
                edge.at[rows], edge_next.at[rows], e_send.at[0, c], e_recv.at[0, c], prv
            )
            copy.start()
            edges_low.append(copy)
        if c >= chunks - edge_chunks:
            e = c - (chunks - edge_chunks)
            edge_rows = slice(e * CHUNK, (e + 1) * CHUNK)
            copy = copy_to(
                edge.at[rows], edge_prev.at[edge_rows], e_send.at[1, e], e_recv.at[1, e], nxt
            )
            copy.start()
            edges_high.append(copy)
        if c % 2 == 0:
            advance(1)
    advance(0)
    sums = [jnp.zeros((1, width), F32) for _ in range(3)]
    for c in range(chunks):
        rows = slice(c * CHUNK, (c + 1) * CHUNK)
        g = own[rows, :]
        if c < edge_chunks:
            before = tok_prev_ref[rows, :]
        else:
            before = tok_ref[(c - edge_chunks) * CHUNK : (c - edge_chunks + 1) * CHUNK, :]
        if c >= chunks - edge_chunks:
            e = c - (chunks - edge_chunks)
            after = tok_next_ref[e * CHUNK : (e + 1) * CHUNK, :]
        else:
            after = tok_ref[(c + edge_chunks) * CHUNK : (c + edge_chunks + 1) * CHUNK, :]
        for n, x in enumerate((before, tok_ref[rows, :], after)):
            sums[n] = sums[n] + jnp.sum(g * x.astype(F32), axis=0, keepdims=True)
    taps_sum[0] = jnp.concatenate(sums + [jnp.zeros((5, width), F32)], axis=0)

    def send_taps(k):
        copy = copy_to(
            taps_sum.at[k], taps_in.at[k], t_send.at[k], t_recv.at[k], partner(bits[k])
        )
        copy.start()
        return copy

    def take_taps(k, copy):
        copy.wait_recv()
        sent.append(copy)
        taps_sum[k + 1] = taps_sum[k] + taps_in[k]

    def finish_tokens():
        for copy in edges_low + edges_high:
            copy.wait_recv()
        for c in range(chunks):
            rows = slice(c * CHUNK, (c + 1) * CHUNK)
            if c < edge_chunks:
                before = edge_prev[rows, :].astype(F32)
            else:
                before = own[(c - edge_chunks) * CHUNK : (c - edge_chunks + 1) * CHUNK, :]
            if c >= chunks - edge_chunks:
                e = c - (chunks - edge_chunks)
                after = edge_next[e * CHUNK : (e + 1) * CHUNK, :].astype(F32)
            else:
                after = own[(c + edge_chunks) * CHUNK : (c + edge_chunks + 1) * CHUNK, :]
            grad_ref[rows, :] = (
                taps_ref[0:1, :] * after + taps_ref[1:2, :] * own[rows, :]
                + taps_ref[2:3, :] * before
            )

    for k in range(stages):
        copy = send_taps(k)
        advance(1)
        advance(0)
        if k == 1:
            finish_tokens()
        take_taps(k, copy)
    if stages < 2:
        finish_tokens()
    for _ in range(2 * stages):
        advance(0)
        advance(1)
    taps_out_ref[...] = taps_sum[stages]
    for copy in sent + parts + edges_low + edges_high:
        copy.wait_send()


def unpack_kernel(final_ref, taps_in_ref, gqw_ref, gkw_ref, gvw_ref, go_ref, taps_ref):
    at = 0
    for out in (gqw_ref, go_ref, gkw_ref, gvw_ref):
        rows = out.shape[0]
        for half in range(out.shape[1] // 128):
            out[:, half * 128 : (half + 1) * 128] = final_ref[at : at + rows, :].astype(F32)
            at += rows
    taps_ref[...] = taps_in_ref[0:3, :]


def body(
    slabs,
    tokens,
    stem_taps,
    query_weight,
    key_weight,
    value_weight,
    out_weight,
    key_blocks,
    counts,
    cotangent,
):
    count, width = tokens.shape
    depth, cols = query_weight.shape
    plane = PLANE_TOK
    sds = jax.ShapeDtypeStruct
    params = pltpu.CompilerParams(vmem_limit_bytes=20 * MIB)
    stages = slabs.bit_length() - 1
    chunks = count // CHUNK
    edge_chunks = plane // CHUNK
    dma = pltpu.SemaphoreType.DMA
    pairs = [(2, edge_chunks)] * 2 + [(chunks,)] * 4 + [(2, edge_chunks)] * 2
    stem, stem_other, cot_other, tok_prev, tok_next, q, ext, grad = pl.pallas_call(
        functools.partial(forward_kernel, slabs),
        out_shape=[
            sds((count, width), BF16),
            sds((count, width), BF16),
            sds((count, width), BF16),
            sds((plane, width), BF16),
            sds((plane, width), BF16),
            sds((count, cols), BF16),
            sds((count + 2 * plane, 2 * cols), BF16),
            sds((count, cols), BF16),
        ],
        in_specs=[VMEM] * 7,
        out_specs=[VMEM] * 8,
        scratch_shapes=[dma(shape) for shape in pairs],
        compiler_params=pltpu.CompilerParams(
            collective_id=0, has_side_effects=True, vmem_limit_bytes=16 * MIB
        ),
    )(tokens, stem_taps, query_weight, key_weight, value_weight, out_weight, cotangent)

    gq, gkv, gprev, gnext, mix, mix_other, gow = pl.pallas_call(
        functools.partial(attention_kernel, slabs),
        out_shape=[
            sds((count, cols), BF16),
            sds((count, 2 * cols), F32),
            sds((plane, 2 * cols), BF16),
            sds((plane, 2 * cols), BF16),
            sds((count, width), F32),
            sds((count, width), BF16),
            sds((cols * depth // 128, 128), F32),
        ],
        in_specs=[SMEM, SMEM] + [VMEM] * 6,
        out_specs=[VMEM] * 7,
        scratch_shapes=[
            pltpu.VMEM((count + 2 * plane, 2 * cols), F32),
            pltpu.VMEM((count, cols), BF16),
        ],
        compiler_params=params,
    )(key_blocks.T, counts, q, ext, grad, cotangent, cot_other, out_weight)
    rows = 4 * depth * cols // 128
    layer_out, grad_tokens, final, taps = pl.pallas_call(
        functools.partial(backward_kernel, slabs),
        out_shape=[
            sds((count, width), BF16),
            sds((count, width), F32),
            sds((rows, 128), BF16),
            sds((8, width), F32),
        ],
        in_specs=[VMEM] * 17,
        out_specs=[VMEM] * 4,
        scratch_shapes=[
            pltpu.VMEM((count, 2 * cols), BF16),
            pltpu.VMEM((plane, 2 * cols), BF16),
            pltpu.VMEM((plane, 2 * cols), BF16),
            pltpu.VMEM((count, width), BF16),
            pltpu.VMEM((count, width), F32),
            pltpu.VMEM((count, width), F32),
            pltpu.VMEM((count, width), BF16),
            pltpu.VMEM((count, width), BF16),
            pltpu.VMEM((count, width), BF16),
            pltpu.VMEM((plane, width), BF16),
            pltpu.VMEM((plane, width), BF16),
            pltpu.VMEM((rows, 128), F32),
            pltpu.VMEM((2, rows // 2, 128), BF16),
            pltpu.VMEM((2, rows // 2, 128), BF16),
            pltpu.VMEM((stages, 8, width), F32),
            pltpu.VMEM((stages + 1, 8, width), F32),
            dma((2,)),
            dma((2,)),
            dma,
            dma,
            dma((chunks,)),
            dma((chunks,)),
            dma((2, edge_chunks)),
            dma((2, edge_chunks)),
            dma((2, 2 * stages)),
            dma((2, 2 * stages)),
            dma((stages,)),
            dma((stages,)),
        ],
        compiler_params=pltpu.CompilerParams(
            collective_id=1, has_side_effects=True, vmem_limit_bytes=30 * MIB
        ),
    )(
        gq,
        gkv,
        gprev,
        gnext,
        stem,
        stem_other,
        query_weight,
        key_weight,
        value_weight,
        gow,
        mix,
        mix_other,
        cotangent,
        tokens,
        tok_prev,
        tok_next,
        stem_taps,
    )
    gqw, gkw, gvw, go, grad_taps = pl.pallas_call(
        unpack_kernel,
        out_shape=[sds((depth, cols), F32)] * 3
        + [sds((cols, depth), F32), sds(stem_taps.shape, F32)],
        in_specs=[VMEM] * 2,
        out_specs=[VMEM] * 5,
        compiler_params=params,
    )(final, taps)
    return (layer_out, grad_tokens, grad_taps, gqw, gkw, gvw, go)


def solution(mesh):
    in_specs = (
        P("slab", "tp"),
        P(None, "tp"),
        P(None, "tp"),
        P(None, "tp"),
        P(None, "tp"),
        P("tp", None),
        P("slab", None),
        P("slab"),
        P("slab", "tp"),
    )
    out_specs = (
        P("slab", "tp"),
        P("slab", "tp"),
        P(None, "tp"),
        P(None, "tp"),
        P(None, "tp"),
        P(None, "tp"),
        P("tp", None),
    )
    return jax.shard_map(
        functools.partial(body, mesh.shape["slab"]),
        mesh=mesh,
        in_specs=in_specs,
        out_specs=out_specs,
        check_vma=False,
    )
```

```python
import functools

import jax
import jax.numpy as jnp
from jax import lax
from jax.experimental import pallas as pl
from jax.experimental.pallas import tpu as pltpu
from jax.sharding import PartitionSpec as P

HD = 64
BLK = 128
PLANE_TOK = 512
MAXK = 4
NEG = -1e30
F32 = jnp.float32
BF16 = jnp.bfloat16
MESH = pl.DeviceIdType.MESH
VMEM = pl.BlockSpec(memory_space=pltpu.VMEM)
SMEM = pl.BlockSpec(memory_space=pltpu.SMEM)
MIB = 1024 * 1024
CHUNK = 256


def mm(a, b):
    return jnp.dot(a, b, preferred_element_type=F32)


def mm_nt(a, b):
    return lax.dot_general(a, b, (((1,), (1,)), ((), ())), preferred_element_type=F32)


def mm_tn(a, b):
    return lax.dot_general(a, b, (((0,), (0,)), ((), ())), preferred_element_type=F32)


def part(index, width):
    return pl.ds(pl.multiple_of(index * width, width), width)


def copy_to(src, dst, send, recv, where):
    return pltpu.make_async_remote_copy(
        src_ref=src,
        dst_ref=dst,
        send_sem=send,
        recv_sem=recv,
        device_id=where,
        device_id_type=MESH,
    )


def forward_kernel(
    slabs,
    all_ref,
    taps_ref,
    ow_ref,
    so_ref,
    st_ref,
    ct_ref,
    prev_ref,
    next_ref,
    q_ref,
    ext_ref,
    grad_ref,
    t_send,
    t_recv,
    s_send,
    s_recv,
    c_send,
    c_recv,
    k_send,
    k_recv,
):
    me = lax.axis_index("slab")
    tp = lax.axis_index("tp")
    tokens, width = so_ref.shape
    cols, depth = ow_ref.shape
    tok_ref = all_ref.at[0:tokens]
    cot_ref = all_ref.at[tokens : 2 * tokens]
    wq_ref, wk_ref, wv_ref = (
        all_ref.at[2 * tokens + n * depth : 2 * tokens + (n + 1) * depth] for n in range(3)
    )
    chunks = tokens // CHUNK
    edge_chunks = PLANE_TOK // CHUNK
    last = tokens - PLANE_TOK
    mine, theirs = part(tp, width), part(1 - tp, width)
    nxt = {"slab": lax.rem(me + 1, slabs)}
    prv = {"slab": lax.rem(me + slabs - 1, slabs)}
    mate = {"tp": 1 - tp}
    barrier = pltpu.get_barrier_semaphore()
    for where in (nxt, prv, mate):
        pl.semaphore_signal(barrier, inc=1, device_id=where, device_id_type=MESH)
    pl.semaphore_wait(barrier, 3)

    def rows_of(c):
        return slice(c * CHUNK, (c + 1) * CHUNK)

    halo = [[], []]
    for e in range(edge_chunks):
        rows = rows_of(e)
        high = slice(last + e * CHUNK, last + (e + 1) * CHUNK)
        up = copy_to(tok_ref.at[high], prev_ref.at[rows], t_send.at[0, e], t_recv.at[0, e], nxt)
        down = copy_to(tok_ref.at[rows], next_ref.at[rows], t_send.at[1, e], t_recv.at[1, e], prv)
        up.start()
        down.start()
        halo[0].append(up)
        halo[1].append(down)
    order = sorted(range(chunks), key=lambda c: (c % edge_chunks, c))
    cots = [
        copy_to(cot_ref.at[rows_of(c)], ct_ref.at[rows_of(c)], c_send.at[c], c_recv.at[c], mate)
        for c in range(chunks)
    ]
    early = chunks // 2
    for c in range(early):
        cots[c].start()
    stems = {}
    for c in order:
        rows = rows_of(c)
        if c < edge_chunks:
            halo[0][c].wait_recv()
            before = prev_ref[rows, :]
        else:
            before = tok_ref[rows_of(c - edge_chunks), :]
        if c >= chunks - edge_chunks:
            e = c - (chunks - edge_chunks)
            halo[1][e].wait_recv()
            after = next_ref[rows_of(e), :]
        else:
            after = tok_ref[rows_of(c + edge_chunks), :]
        so_ref[rows, :] = (
            taps_ref[0:1, :] * before.astype(F32)
            + taps_ref[1:2, :] * tok_ref[rows, :].astype(F32)
            + taps_ref[2:3, :] * after.astype(F32)
        ).astype(BF16)
        stems[c] = copy_to(so_ref.at[rows], st_ref.at[rows], s_send.at[c], s_recv.at[c], mate)
        stems[c].start()
    for c in range(early, chunks):
        cots[c].start()

    def output_gradient(c):
        rows = rows_of(c)
        cots[c].wait_recv()
        grad_ref[rows, :] = (
            mm_nt(cot_ref[rows, :], ow_ref[:, mine]) + mm_nt(ct_ref[rows, :], ow_ref[:, theirs])
        ).astype(BF16)

    for c in range(early):
        output_gradient(c)
    edges = []
    for c in order:
        rows = rows_of(c)
        stems[c].wait_recv()
        so, st = so_ref[rows, :], st_ref[rows, :]

        def project(w_ref):
            return (mm(so, w_ref[mine, :]) + mm(st, w_ref[theirs, :])).astype(BF16)

        place = slice(PLANE_TOK + c * CHUNK, PLANE_TOK + (c + 1) * CHUNK)
        ext_ref[place, 0:cols] = project(wk_ref)
        ext_ref[place, cols : 2 * cols] = project(wv_ref)
        if c < edge_chunks:
            at = PLANE_TOK + tokens + c * CHUNK
            copy = copy_to(
                ext_ref.at[place],
                ext_ref.at[at : at + CHUNK],
                k_send.at[0, c],
                k_recv.at[0, c],
                prv,
            )
            copy.start()
            edges.append(copy)
        if c >= chunks - edge_chunks:
            e = c - (chunks - edge_chunks)
            copy = copy_to(
                ext_ref.at[place],
                ext_ref.at[rows_of(e)],
                k_send.at[1, e],
                k_recv.at[1, e],
                nxt,
            )
            copy.start()
            edges.append(copy)
        q_ref[rows, :] = project(wq_ref)
    for c in range(early, chunks):
        output_gradient(c)
    for copy in edges:
        copy.wait_recv()
    for copy in halo[0] + halo[1] + cots + list(stems.values()) + edges:
        copy.wait_send()


def attention_kernel(
    slabs,
    blocks_ref,
    counts_ref,
    q_ref,
    ext,
    grad,
    co_ref,
    ct_ref,
    ow_ref,
    gq_ref,
    gkv_ref,
    gprev_ref,
    gnext_ref,
    mix_ref,
    mix_other_ref,
    gow_ref,
    acc,
    attn,
):
    tp = lax.axis_index("tp")
    slab = lax.axis_index("slab")
    tokens, cols = q_ref.shape
    width = co_ref.shape[1]
    heads = cols // HD
    planes = tokens // PLANE_TOK
    per_plane = PLANE_TOK // BLK
    total = planes * slabs
    mine, other = part(tp, width), part(1 - tp, width)

    @pl.loop(0, acc.shape[0] // BLK)
    def _(step):
        acc[part(step, BLK), :] = jnp.zeros((BLK, 2 * cols), F32)

    lane = lax.broadcasted_iota(jnp.int32, (1, cols), 1) // HD
    masks = [(lane == h).astype(F32).astype(BF16) for h in range(heads)]

    def stack(block):
        return jnp.concatenate([block * mask for mask in masks], axis=0)

    def pick(value):
        heads_t = [
            value[h * HD : (h + 1) * HD, h * BLK : (h + 1) * BLK] for h in range(heads)
        ]
        return jnp.concatenate(heads_t, axis=0).T

    @pl.loop(0, tokens // BLK)
    def _(i):
        rows = part(i, BLK)
        where = []
        for j in range(MAXK):
            block = blocks_ref[j, i]
            plane = lax.rem(
                lax.div(block, per_plane) - slab * planes + 1 + total, total
            )
            where.append(part(plane * per_plane + lax.rem(block, per_plane), BLK))
        keys = jnp.concatenate([ext[at, 0:cols] for at in where], axis=0)
        values = jnp.concatenate([ext[at, cols : 2 * cols] for at in where], axis=0)
        queries = stack(q_ref[rows, :] * jnp.asarray(HD**-0.5, BF16))
        grads = stack(grad[rows, :])
        scores = mm_nt(keys, queries)
        live = counts_ref[i]
        scores = jnp.concatenate(
            [
                jnp.where(j < live, scores[j * BLK : (j + 1) * BLK], NEG)
                for j in range(MAXK)
            ],
            axis=0,
        )
        exps = jnp.exp(scores - jnp.max(scores, axis=0, keepdims=True))
        probs = exps * (1.0 / jnp.sum(exps, axis=0, keepdims=True))
        low = probs.astype(BF16)
        attn[rows, :] = pick(mm_tn(values, low)).astype(BF16)
        gprobs = mm_nt(values, grads)
        inner = jnp.sum(probs * gprobs, axis=0, keepdims=True)
        gscores = (probs * (gprobs - inner)).astype(BF16)
        gq_ref[rows, :] = (pick(mm_tn(keys, gscores)) * (HD**-0.5)).astype(BF16)
        gkeys = mm(gscores, queries)
        gvalues = mm(low, grads)
        for j in range(MAXK):
            acc[where[j], 0:cols] += gkeys[j * BLK : (j + 1) * BLK]
            acc[where[j], cols : 2 * cols] += gvalues[j * BLK : (j + 1) * BLK]

    gprev_ref[...] = acc[0:PLANE_TOK, :].astype(BF16)
    gkv_ref[...] = acc[PLANE_TOK : PLANE_TOK + tokens, :]
    gnext_ref[...] = acc[PLANE_TOK + tokens : 2 * PLANE_TOK + tokens, :].astype(BF16)

    @pl.loop(0, tokens // CHUNK)
    def _(step):
        rows = part(step, CHUNK)
        mix_ref[rows, :] = mm(attn[rows, :], ow_ref[:, mine])
        mix_other_ref[rows, :] = mm(attn[rows, :], ow_ref[:, other]).astype(BF16)

    halves = width // 128
    for index, c_ref in ((tp, co_ref), (1 - tp, ct_ref)):
        product = mm_tn(attn[...], c_ref[...])
        for half in range(halves):
            gow_ref[part(index * halves + half, cols), :] = product[
                :, half * 128 : (half + 1) * 128
            ]


def backward_kernel(
    slabs,
    gq_ref,
    gkv_ref,
    gprev_ref,
    gnext_ref,
    so_ref,
    st_ref,
    wq_ref,
    wk_ref,
    wv_ref,
    gow_ref,
    mix_ref,
    mix_other_ref,
    cot_ref,
    tok_ref,
    tok_prev_ref,
    tok_next_ref,
    taps_ref,
    layer_ref,
    grad_ref,
    final,
    taps_out_ref,
    low,
    from_prev,
    from_next,
    mix_in,
    own,
    other,
    part_out,
    part_in,
    edge,
    edge_prev,
    edge_next,
    acc,
    outgoing,
    incoming,
    taps_in,
    taps_sum,
    h_send,
    h_recv,
    m_send,
    m_recv,
    p_send,
    p_recv,
    e_send,
    e_recv,
    s_send,
    s_recv,
    t_send,
    t_recv,
):
    me = lax.axis_index("slab")
    tp = lax.axis_index("tp")
    bits = tuple(range(slabs.bit_length() - 1))
    stages = len(bits)
    orders = (bits[:1] + bits[2:] + bits[1:2], bits)
    tokens, cols = gq_ref.shape
    width = so_ref.shape[1]
    depth = wq_ref.shape[0]
    halves = cols // 128
    span = acc.shape[0] // 2
    last = tokens - PLANE_TOK
    chunks = tokens // CHUNK
    edge_chunks = PLANE_TOK // CHUNK
    mine, theirs = part(tp, width), part(1 - tp, width)
    nxt = {"slab": lax.rem(me + 1, slabs)}
    prv = {"slab": lax.rem(me + slabs - 1, slabs)}
    mate = {"tp": 1 - tp}

    def bit_of(b):
        return lax.rem(lax.div(me, 1 << b), 2)

    def partner(b):
        return {"slab": me + (1 - 2 * bit_of(b)) * (1 << b)}

    barrier = pltpu.get_barrier_semaphore()
    for where in [partner(b) for b in bits] + [nxt, prv, mate]:
        pl.semaphore_signal(barrier, inc=1, device_id=where, device_id_type=MESH)
    pl.semaphore_wait(barrier, stages + 3)

    down = copy_to(gprev_ref, from_next, h_send.at[0], h_recv.at[0], prv)
    up = copy_to(gnext_ref, from_prev, h_send.at[1], h_recv.at[1], nxt)
    mix_copy = copy_to(mix_other_ref, mix_in, m_send, m_recv, mate)
    down.start()
    up.start()
    mix_copy.start()
    sent = [down, up, mix_copy]

    lows = [jnp.int32(0), jnp.int32(span)]
    trail = [[], []]
    step_of = [0, 0]
    flight = [None, None]

    def rows_at(at, size):
        return pl.ds(pl.multiple_of(at, 16), size)

    def advance(t):
        k = step_of[t]
        if k > 2 * stages:
            return
        if flight[t] is not None:
            flight[t].wait_recv()
            sent.append(flight[t])
            if k <= stages:
                size = span >> k
                at = rows_at(lows[t], size)
                offset = span - 2 * size
                acc[at, :] = acc[at, :] + incoming[t, pl.ds(offset, size), :].astype(F32)
        if k == stages:
            at = rows_at(lows[t], span >> stages)
            final[at, :] = acc[at, :].astype(BF16)
        if k < stages:
            size = span >> (k + 1)
            b = orders[t][k]
            bit = bit_of(b)
            keep = lows[t] + bit * size
            give = lows[t] + (1 - bit) * size
            slots = pl.ds(span - 2 * size, size)
            outgoing[t, slots, :] = acc[rows_at(give, size), :].astype(BF16)
            flight[t] = copy_to(
                outgoing.at[t, slots],
                incoming.at[t, slots],
                s_send.at[t, k],
                s_recv.at[t, k],
                partner(b),
            )
            flight[t].start()
            lows[t] = keep
            trail[t].append(keep)
        elif k < 2 * stages:
            j = 2 * stages - 1 - k
            at = rows_at(trail[t][j], span >> (j + 1))
            flight[t] = copy_to(
                final.at[at],
                final.at[at],
                s_send.at[t, k],
                s_recv.at[t, k],
                partner(orders[t][j]),
            )
            flight[t].start()
        step_of[t] = k + 1

    def weight_gradient(base, g):
        for index, s_ref in ((tp, so_ref), (1 - tp, st_ref)):
            product = mm_tn(s_ref[...], g)
            for half in range(halves):
                at = pl.multiple_of(base + half * depth + index * width, 128)
                acc[pl.ds(at, width), :] = product[:, half * 128 : (half + 1) * 128]

    block = depth * halves
    weight_gradient(0, gq_ref[...])
    acc[block : 2 * block, :] = gow_ref[...]
    advance(0)
    for c in range(chunks):
        rows = slice(c * CHUNK, (c + 1) * CHUNK)
        gq = gq_ref[rows, :]
        own[rows, :] = mm_nt(gq, wq_ref[mine, :])
        other[rows, :] = mm_nt(gq, wq_ref[theirs, :])
    advance(0)
    advance(0)
    down.wait_recv()
    up.wait_recv()
    parts = []
    for c in range(chunks):
        rows = slice(c * CHUNK, (c + 1) * CHUNK)
        total = gkv_ref[rows, :]
        if c < edge_chunks:
            total = total + from_prev[rows, :].astype(F32)
        if c >= chunks - edge_chunks:
            edge_rows = slice(c * CHUNK - last, (c + 1) * CHUNK - last)
            total = total + from_next[edge_rows, :].astype(F32)
        total = total.astype(BF16)
        low[rows, :] = total
        gk, gv = total[:, :cols], total[:, cols:]
        part_out[rows, :] = (
            other[rows, :] + mm_nt(gk, wk_ref[theirs, :]) + mm_nt(gv, wv_ref[theirs, :])
        ).astype(BF16)
        copy = copy_to(part_out.at[rows], part_in.at[rows], p_send.at[c], p_recv.at[c], mate)
        copy.start()
        parts.append(copy)
        own[rows, :] += mm_nt(gk, wk_ref[mine, :]) + mm_nt(gv, wv_ref[mine, :])
    advance(0)
    weight_gradient(2 * block, low[:, :cols])
    weight_gradient(3 * block, low[:, cols:])
    advance(1)
    advance(0)
    advance(1)
    mix_copy.wait_recv()
    layer_ref[...] = (
        so_ref[...].astype(F32) + (mix_ref[...] + mix_in[...].astype(F32))
    ).astype(BF16)
    advance(0)
    edges_low, edges_high = [], []
    for c in range(chunks):
        rows = slice(c * CHUNK, (c + 1) * CHUNK)
        parts[c].wait_recv()
        stem_grad = cot_ref[rows, :].astype(F32) + (own[rows, :] + part_in[rows, :].astype(F32))
        own[rows, :] = stem_grad
        edge[rows, :] = stem_grad.astype(BF16)
        if c < edge_chunks:
            copy = copy_to(
                edge.at[rows], edge_next.at[rows], e_send.at[0, c], e_recv.at[0, c], prv
            )
            copy.start()
            edges_low.append(copy)
        if c >= chunks - edge_chunks:
            e = c - (chunks - edge_chunks)
            edge_rows = slice(e * CHUNK, (e + 1) * CHUNK)
            copy = copy_to(
                edge.at[rows], edge_prev.at[edge_rows], e_send.at[1, e], e_recv.at[1, e], nxt
            )
            copy.start()
            edges_high.append(copy)
        if c % 2 == 0:
            advance(1)
    advance(0)
    sums = [jnp.zeros((1, width), F32) for _ in range(3)]
    for c in range(chunks):
        rows = slice(c * CHUNK, (c + 1) * CHUNK)
        g = own[rows, :]
        if c < edge_chunks:
            before = tok_prev_ref[rows, :]
        else:
            before = tok_ref[(c - edge_chunks) * CHUNK : (c - edge_chunks + 1) * CHUNK, :]
        if c >= chunks - edge_chunks:
            e = c - (chunks - edge_chunks)
            after = tok_next_ref[e * CHUNK : (e + 1) * CHUNK, :]
        else:
            after = tok_ref[(c + edge_chunks) * CHUNK : (c + edge_chunks + 1) * CHUNK, :]
        for n, x in enumerate((before, tok_ref[rows, :], after)):
            sums[n] = sums[n] + jnp.sum(g * x.astype(F32), axis=0, keepdims=True)
    taps_sum[0] = jnp.concatenate(sums + [jnp.zeros((5, width), F32)], axis=0)

    def send_taps(k):
        copy = copy_to(
            taps_sum.at[k], taps_in.at[k], t_send.at[k], t_recv.at[k], partner(bits[k])
        )
        copy.start()
        return copy

    def take_taps(k, copy):
        copy.wait_recv()
        sent.append(copy)
        taps_sum[k + 1] = taps_sum[k] + taps_in[k]

    def finish_tokens():
        for copy in edges_low + edges_high:
            copy.wait_recv()
        for c in range(chunks):
            rows = slice(c * CHUNK, (c + 1) * CHUNK)
            if c < edge_chunks:
                before = edge_prev[rows, :].astype(F32)
            else:
                before = own[(c - edge_chunks) * CHUNK : (c - edge_chunks + 1) * CHUNK, :]
            if c >= chunks - edge_chunks:
                e = c - (chunks - edge_chunks)
                after = edge_next[e * CHUNK : (e + 1) * CHUNK, :].astype(F32)
            else:
                after = own[(c + edge_chunks) * CHUNK : (c + edge_chunks + 1) * CHUNK, :]
            grad_ref[rows, :] = (
                taps_ref[0:1, :] * after + taps_ref[1:2, :] * own[rows, :]
                + taps_ref[2:3, :] * before
            )

    for k in range(stages):
        copy = send_taps(k)
        advance(1)
        advance(0)
        if k == 1:
            finish_tokens()
        take_taps(k, copy)
    if stages < 2:
        finish_tokens()
    for _ in range(2 * stages):
        advance(0)
        advance(1)
    taps_out_ref[...] = taps_sum[stages]
    for copy in sent + parts + edges_low + edges_high:
        copy.wait_send()


def unpack_kernel(final_ref, taps_in_ref, gqw_ref, gkw_ref, gvw_ref, go_ref, taps_ref):
    at = 0
    for out in (gqw_ref, go_ref, gkw_ref, gvw_ref):
        rows = out.shape[0]
        for half in range(out.shape[1] // 128):
            out[:, half * 128 : (half + 1) * 128] = final_ref[at : at + rows, :].astype(F32)
            at += rows
    taps_ref[...] = taps_in_ref[0:3, :]


def body(
    slabs,
    tokens,
    stem_taps,
    query_weight,
    key_weight,
    value_weight,
    out_weight,
    key_blocks,
    counts,
    cotangent,
):
    count, width = tokens.shape
    depth, cols = query_weight.shape
    plane = PLANE_TOK
    sds = jax.ShapeDtypeStruct
    params = pltpu.CompilerParams(vmem_limit_bytes=20 * MIB)
    stages = slabs.bit_length() - 1
    chunks = count // CHUNK
    edge_chunks = plane // CHUNK
    dma = pltpu.SemaphoreType.DMA
    pairs = [(2, edge_chunks)] * 2 + [(chunks,)] * 4 + [(2, edge_chunks)] * 2
    stem, stem_other, cot_other, tok_prev, tok_next, q, ext, grad = pl.pallas_call(
        functools.partial(forward_kernel, slabs),
        out_shape=[
            sds((count, width), BF16),
            sds((count, width), BF16),
            sds((count, width), BF16),
            sds((plane, width), BF16),
            sds((plane, width), BF16),
            sds((count, cols), BF16),
            sds((count + 2 * plane, 2 * cols), BF16),
            sds((count, cols), BF16),
        ],
        in_specs=[VMEM] * 3,
        out_specs=[VMEM] * 8,
        scratch_shapes=[dma(shape) for shape in pairs],
        compiler_params=pltpu.CompilerParams(
            collective_id=0, has_side_effects=True, vmem_limit_bytes=16 * MIB
        ),
    )(
        jnp.concatenate([tokens, cotangent, query_weight, key_weight, value_weight]),
        stem_taps,
        out_weight,
    )

    gq, gkv, gprev, gnext, mix, mix_other, gow = pl.pallas_call(
        functools.partial(attention_kernel, slabs),
        out_shape=[
            sds((count, cols), BF16),
            sds((count, 2 * cols), F32),
            sds((plane, 2 * cols), BF16),
            sds((plane, 2 * cols), BF16),
            sds((count, width), F32),
            sds((count, width), BF16),
            sds((cols * depth // 128, 128), F32),
        ],
        in_specs=[SMEM, SMEM] + [VMEM] * 6,
        out_specs=[VMEM] * 7,
        scratch_shapes=[
            pltpu.VMEM((count + 2 * plane, 2 * cols), F32),
            pltpu.VMEM((count, cols), BF16),
        ],
        compiler_params=params,
    )(key_blocks.T, counts, q, ext, grad, cotangent, cot_other, out_weight)
    rows = 4 * depth * cols // 128
    layer_out, grad_tokens, final, taps = pl.pallas_call(
        functools.partial(backward_kernel, slabs),
        out_shape=[
            sds((count, width), BF16),
            sds((count, width), F32),
            sds((rows, 128), BF16),
            sds((8, width), F32),
        ],
        in_specs=[VMEM] * 17,
        out_specs=[VMEM] * 4,
        scratch_shapes=[
            pltpu.VMEM((count, 2 * cols), BF16),
            pltpu.VMEM((plane, 2 * cols), BF16),
            pltpu.VMEM((plane, 2 * cols), BF16),
            pltpu.VMEM((count, width), BF16),
            pltpu.VMEM((count, width), F32),
            pltpu.VMEM((count, width), F32),
            pltpu.VMEM((count, width), BF16),
            pltpu.VMEM((count, width), BF16),
            pltpu.VMEM((count, width), BF16),
            pltpu.VMEM((plane, width), BF16),
            pltpu.VMEM((plane, width), BF16),
            pltpu.VMEM((rows, 128), F32),
            pltpu.VMEM((2, rows // 2, 128), BF16),
            pltpu.VMEM((2, rows // 2, 128), BF16),
            pltpu.VMEM((stages, 8, width), F32),
            pltpu.VMEM((stages + 1, 8, width), F32),
            dma((2,)),
            dma((2,)),
            dma,
            dma,
            dma((chunks,)),
            dma((chunks,)),
            dma((2, edge_chunks)),
            dma((2, edge_chunks)),
            dma((2, 2 * stages)),
            dma((2, 2 * stages)),
            dma((stages,)),
            dma((stages,)),
        ],
        compiler_params=pltpu.CompilerParams(
            collective_id=1, has_side_effects=True, vmem_limit_bytes=30 * MIB
        ),
    )(
        gq,
        gkv,
        gprev,
        gnext,
        stem,
        stem_other,
        query_weight,
        key_weight,
        value_weight,
        gow,
        mix,
        mix_other,
        cotangent,
        tokens,
        tok_prev,
        tok_next,
        stem_taps,
    )
    gqw, gkw, gvw, go, grad_taps = pl.pallas_call(
        unpack_kernel,
        out_shape=[sds((depth, cols), F32)] * 3
        + [sds((cols, depth), F32), sds(stem_taps.shape, F32)],
        in_specs=[VMEM] * 2,
        out_specs=[VMEM] * 5,
        compiler_params=params,
    )(final, taps)
    return (layer_out, grad_tokens, grad_taps, gqw, gkw, gvw, go)


def solution(mesh):
    in_specs = (
        P("slab", "tp"),
        P(None, "tp"),
        P(None, "tp"),
        P(None, "tp"),
        P(None, "tp"),
        P("tp", None),
        P("slab", None),
        P("slab"),
        P("slab", "tp"),
    )
    out_specs = (
        P("slab", "tp"),
        P("slab", "tp"),
        P(None, "tp"),
        P(None, "tp"),
        P(None, "tp"),
        P(None, "tp"),
        P("tp", None),
    )
    return jax.shard_map(
        functools.partial(body, mesh.shape["slab"]),
        mesh=mesh,
        in_specs=in_specs,
        out_specs=out_specs,
        check_vma=False,
    )
```
